128 devices in a mesh: row: 8 (over z, core), col: 16 (over y, x).
Axes of the slice: x: 4, y: 4, z: 4, core: 2. Of those that a mesh axis runs over, the one named last changes fastest.
Arguments:
- tile_u: bfloat16 [64, 16, 2048, 128], P('row', 'col'), may hold values from -6 to 6
- tile_v: bfloat16 [64, 16, 2048, 128], P('row', 'col'), may hold values from -0.5 to 0.5
- tile_rank: int32 [64, 16], P('row', 'col'), may hold values from 16 to 128, as said below
- listed: int32 [64, 16], P('row', 'col'), may hold values from 0 to 1, as said below
- row_u: bfloat16 [64, 2048, 128], P('row', 'col'), may hold values from -6 to 6
- row_v: bfloat16 [64, 2048, 128], P('row', 'col'), may hold values from -0.5 to 0.5
- row_rank: int32 [64], P('row'), may hold values from 16 to 128
- col_u: bfloat16 [16, 2048, 128], P('col', 'row'), may hold values from -6 to 6
- col_v: bfloat16 [16, 2048, 128], P('col', 'row'), may hold values from -0.5 to 0.5
- col_rank: int32 [16], P('col'), may hold values from 16 to 112
- sketch: bfloat16 [2048, 128], replicated, may hold values from -0.125 to 0.125
Outputs:
- out_u: bfloat16 [64, 16, 2048, 128], P('row', 'col')
- out_v: bfloat16 [64, 16, 2048, 128], P('row', 'col')
The draws below stay inside these ranges and needn't reach their ends.
Inputs may be any that keep to these rules, and one draw needn't show every extreme that they name: A tile with listed 0 has tile_rank plus the col_rank of its column at most 128; a tile with listed 1 has more than 128. The tiles of one device are tile rows a * 8 to a * 8 + 7 and tile columns b * 1 to b + 1 - 1 for its indices a along row and b along col. Two devices of the same row index whose col indices differ by 8 hold together at most 8 listed tiles; some device holds 8.
All inputs are finite; a program needn't handle non-finite values.
Results may differ from the reference program's by a relative error of at most 0.0072.
Values may be sent and summed in bfloat16 or wider, within the bound.
A program may use at most 192 MiB of HBM per device.

```python
import jax
import jax.numpy as jnp
from jax import lax

B = 2048
R = 128
S = 128
TR = 8
TC = 1
NTR = 64
NTC = 16
N_ROW = 8
N_COL = 16


def joint_ranks(key):
    base = jax.random.fold_in(key, 41)
    keys = jax.random.split(base, 7)
    col_rank = jax.random.randint(keys[0], (NTC,), R // 8, R - R // 8 + 1)
    capacity = TR * TC
    pairs = N_COL // 2
    first = jax.random.randint(keys[1], (N_ROW, pairs), 0, capacity + 1)
    corner = (lax.broadcasted_iota(jnp.int32, (N_ROW, pairs), 0) == 0) & (lax.broadcasted_iota(jnp.int32, (N_ROW, pairs), 1) == 0)
    first = jnp.where(corner, capacity, first)
    second = jax.random.randint(keys[2], (N_ROW, pairs), 0, capacity - first + 1)
    flipped = jax.random.randint(keys[3], (N_ROW, pairs), 0, 2)
    lower_half = jnp.where(flipped == 1, second, first)
    upper_half = jnp.where(flipped == 1, first, second)
    counts = jnp.concatenate([lower_half, upper_half], axis=1)
    perm_keys = jax.random.split(keys[4], N_ROW * N_COL)
    orders = jax.vmap(lambda single: jax.random.permutation(single, capacity))(perm_keys)
    orders = orders.reshape(N_ROW, N_COL, capacity)
    listed = (orders < counts[:, :, None]).astype(jnp.int32)
    listed = listed.reshape(N_ROW, N_COL, TR, TC).transpose(0, 2, 1, 3).reshape(NTR, NTC)
    column = jnp.broadcast_to(col_rank[None, :], (NTR, NTC))
    high_floor = jnp.maximum(S - column + 1, R // 8)
    high_rank = jax.random.randint(keys[5], (NTR, NTC), high_floor, R + 1)
    low_rank = jax.random.randint(keys[6], (NTR, NTC), R // 8, S - column + 1)
    tile_rank = jnp.where(listed == 1, high_rank, low_rank).astype(jnp.int32)
    return (col_rank.astype(jnp.int32), listed, tile_rank)


def draw_tile_rank(key, part):
    return joint_ranks(key)[2]


def draw_listed(key, part):
    return joint_ranks(key)[1]


def draw_col_rank(key, part):
    return joint_ranks(key)[0]


def with_ends(result, own_key, low, top_value):
    longest = result.shape.index(max(result.shape))
    spots = []
    for shift in (0, 1):
        where = [jax.random.randint(jax.random.fold_in(own_key, axis), (), 0, length) for axis, length in enumerate(result.shape)]
        where[longest] = (where[longest] + shift) % result.shape[longest]
        spots.append(tuple(where))
    return result.at[spots[0]].set(low).at[spots[1]].set(top_value)


def shard_levels(own_key, dims, cuts, low, high):
    level = 1.0
    for position, parts in cuts:
        steps = jax.random.uniform(jax.random.fold_in(jax.random.fold_in(own_key, 6), position), (parts,), jnp.float32, low / len(cuts), high / len(cuts))
        level = level * jnp.repeat(jnp.exp(steps), dims[position] // parts).reshape((-1,) + (1,) * (len(dims) - 1 - position))
    return level


def centred(stream_key, dims, deviation, bound, pieces=(), held_as=jnp.bfloat16):
    gain = shard_levels(stream_key, dims, pieces, -0.22, 0.18) if pieces else 1.0
    entries = jax.random.normal(stream_key, dims, jnp.float32) * deviation * gain
    return jnp.minimum(jnp.maximum(entries, -bound), bound).astype(held_as)


def setup_inputs(seed: int = 0) -> dict:
    seeds = jax.random.split(jax.random.key(seed), 12)
    tile_u = centred(seeds[0], (NTR, NTC, B, R), 1.0, 6.0, ((0, 8), (1, 16)))
    tile_v = centred(seeds[1], (NTR, NTC, B, R), R ** -0.5, 0.5, ((0, 8), (1, 16)))
    tile_rank = draw_tile_rank(jax.random.fold_in(seeds[11], 71), 0)
    listed = draw_listed(jax.random.fold_in(seeds[11], 71), 0)
    row_u = centred(seeds[4], (NTR, B, R), 1.0, 6.0, ((0, 8), (1, 16)))
    row_v = centred(seeds[5], (NTR, B, R), R ** -0.5, 0.5, ((0, 8), (1, 16)))
    row_rank = with_ends(jax.random.randint(seeds[6], (NTR,), R // 8, R + 1), jax.random.fold_in(seeds[6], 1), R // 8, R).astype(jnp.int32)
    col_u = centred(seeds[7], (NTC, B, R), 1.0, 6.0, ((0, 16), (1, 8)))
    col_v = centred(seeds[8], (NTC, B, R), R ** -0.5, 0.5, ((0, 16), (1, 8)))
    col_rank = draw_col_rank(jax.random.fold_in(seeds[11], 71), 0)
    sketch = centred(seeds[10], (B, S), B ** -0.5, 0.125)
    return {"tile_u": tile_u, "tile_v": tile_v, "tile_rank": tile_rank, "listed": listed, "row_u": row_u, "row_v": row_v, "row_rank": row_rank, "col_u": col_u, "col_v": col_v, "col_rank": col_rank, "sketch": sketch}


def masked(factor, rank):
    width = factor.shape[-1]
    keep = lax.broadcasted_iota(jnp.int32, (width,), 0) < rank[..., None]
    return factor * keep[..., None, :].astype(factor.dtype)

def shifted(block, rank):
    width = block.shape[-1]
    target = lax.broadcasted_iota(jnp.int32, (width, width), 1)
    source = lax.broadcasted_iota(jnp.int32, (width, width), 0)
    shift = (target[None] == source[None] + rank[:, None, None]).astype(jnp.float32)
    return jnp.einsum('jbr,jrc->jbc', block.astype(jnp.float32), shift)

def update_row(tile_u, tile_v, ranks, flags, pan_u, pan_v, col_u, col_v, sketch):
    f32 = jnp.float32
    core = jnp.einsum('br,jbs->jrs', pan_v.astype(f32), col_v.astype(f32)).astype(jnp.bfloat16)
    left = jnp.einsum('br,jrs->jbs', pan_u.astype(f32), core.astype(f32)).astype(jnp.bfloat16)
    plain_u = (tile_u.astype(f32) + shifted(left, ranks)).astype(jnp.bfloat16)
    plain_v = (tile_v.astype(f32) - shifted(col_u, ranks)).astype(jnp.bfloat16)
    unew = jnp.concatenate([tile_u, left], axis=-1)
    vnew = jnp.concatenate([tile_v, -col_u], axis=-1)
    proj = jnp.einsum('jbq,bs->jqs', vnew.astype(f32), sketch.astype(f32)).astype(jnp.bfloat16)
    span = jnp.einsum('jbq,jqs->jbs', unew.astype(f32), proj.astype(f32))
    gram = jnp.einsum('jbs,jbt->jst', span, span, precision=lax.Precision.HIGHEST)
    width = gram.shape[-1]
    level = jnp.trace(gram, axis1=1, axis2=2) / width
    eye = jnp.eye(width, dtype=jnp.float32)
    gram = gram + (0.01 * level + 1e-06)[:, None, None] * eye
    factor = jnp.linalg.cholesky(gram)
    basis = lax.linalg.triangular_solve(factor, span, left_side=False, lower=True, transpose_a=True)
    order = span.shape[1]
    new_u = (basis * jnp.sqrt(jnp.float32(order))).astype(jnp.bfloat16)
    coef = (jnp.einsum('jbq,jbs->jqs', unew.astype(f32), new_u.astype(f32)) / order).astype(jnp.bfloat16)
    new_v = jnp.einsum('jbq,jqs->jbs', vnew.astype(f32), coef.astype(f32)).astype(jnp.bfloat16)
    pick = flags[:, None, None] == 1
    return (jnp.where(pick, new_u, plain_u), jnp.where(pick, new_v, plain_v))

def reference(tile_u, tile_v, tile_rank, listed, row_u, row_v, row_rank, col_u, col_v, col_rank, sketch):
    tile_u = masked(tile_u, tile_rank)
    tile_v = masked(tile_v, tile_rank)
    row_u = masked(row_u, row_rank)
    row_v = masked(row_v, row_rank)
    col_u = masked(col_u, col_rank)
    col_v = masked(col_v, col_rank)

    def one_row(items):
        return update_row(items[0], items[1], items[2], items[3], items[4], items[5], col_u, col_v, sketch)
    return lax.map(one_row, (tile_u, tile_v, tile_rank, listed, row_u, row_v))
```

```python
import functools

import jax
import jax.numpy as jnp
from jax import lax
from jax.experimental import pallas as pl
from jax.experimental.pallas import tpu as pltpu
from jax.sharding import PartitionSpec as P

f32 = jnp.float32
bf16 = jnp.bfloat16
NB = 32


def tdot(a, b):
    return lax.dot_general(a, b, (((0,), (0,)), ((), ())), preferred_element_type=f32)


def ndot(a, b):
    return lax.dot_general(a, b, (((1,), (0,)), ((), ())), preferred_element_type=f32)


def split(x):
    hi = x.astype(bf16)
    return hi, (x - hi.astype(f32)).astype(bf16)


def iota(shape, dim):
    return lax.broadcasted_iota(jnp.int32, shape, dim)


def front_kernel(trank, rrank, crank, q_ref, p_ref, u_ref, v_ref, y_ref, x_ref, s_ref, m_ref, a_ref, left_ref, px_ref):
    i = pl.program_id(0)
    w = u_ref.shape[-1]
    core = tdot(q_ref[0], y_ref[0])
    r, c = iota((w, w), 0), iota((w, w), 1)
    core = jnp.where((r < rrank[i]) & (c < crank[0]), core, 0.0).astype(bf16)
    proj = tdot(v_ref[0], s_ref[...])
    a_ref[0] = jnp.where(r < trank[i], proj, 0.0).astype(bf16)
    left = ndot(p_ref[0], core).astype(bf16)
    left_ref[0] = left
    both = jnp.concatenate([u_ref[0], left], axis=1)
    m_ref[0] = tdot(both, both)

    @pl.when(i == 0)
    def _():
        px = tdot(x_ref[0], s_ref[...])
        px_ref[...] = jnp.where(r < crank[0], -px, 0.0).astype(bf16)


def eliminate(f_ref, nt, w):
    lane3 = iota((1, 1, w), 2)
    sub3 = iota((1, 8, 1), 1)
    lane2, row2 = iota((NB, w), 1), iota((NB, w), 0)
    for p in range(w // NB):
        r0 = NB * p
        parts = [f_ref[:, r0 + 8 * q : r0 + 8 * q + 8, :] for q in range(NB // 8)]
        for k in range(NB):
            c, q0, s = r0 + k, k // 8, k % 8
            cols = [jnp.broadcast_to(parts[q][:, :, c : c + 1], (nt, 8, w)) for q in range(q0, NB // 8)]
            inv = 1.0 / cols[0][:, s : s + 1, :]
            row = parts[q0][:, s : s + 1, :]
            row = jnp.where(lane3 == c, 1.0, row) * inv
            for q in range(q0, NB // 8):
                col, here = cols[q - q0], lane3 == c
                if q == q0:
                    col = jnp.where(sub3 > s, col, 0.0)
                    here = here & (sub3 > s)
                parts[q] = jnp.where(here, 0.0, parts[q]) - col * row
        for q in range(NB // 8):
            f_ref[:, r0 + 8 * q : r0 + 8 * q + 8, :] = parts[q]
        if r0 + NB < w:
            for t in range(nt):
                panel = f_ref[t, r0 : r0 + NB, :]
                diag = jnp.sum(jnp.where(lane2 == row2 + r0, panel, 0.0), axis=1, keepdims=True)
                mult = panel * (1.0 / diag)
                inside = (lane2 >= r0) & (lane2 < r0 + NB)
                unit = jnp.where(lane2 - r0 < row2, panel, jnp.where(lane2 - r0 == row2, 1.0, 0.0))
                rhs = jnp.where(inside, unit, panel)
                upd = lax.dot_general(
                    mult, rhs, (((0,), (0,)), ((), ())), preferred_element_type=f32, precision=lax.Precision.HIGHEST
                )[r0 + NB :, :]
                old = f_ref[t, r0 + NB :, :]
                lane = iota(old.shape, 1)
                old = jnp.where((lane >= r0) & (lane < r0 + NB), 0.0, old)
                f_ref[t, r0 + NB :, :] = old - upd


def bt(a, b):
    return lax.dot_general(a, b, (((1,), (1,)), ((), ())), preferred_element_type=f32)


def mid_kernel(order, trank, crank, listed, m_ref, a_ref, px_ref, z_ref, rv_ref, f_ref, t_ref):
    nt, w = a_ref.shape[0], a_ref.shape[-1]
    r, c = iota((w, w), 0), iota((w, w), 1)
    for t in range(nt):
        cmat = jnp.concatenate([a_ref[t], px_ref[...]], axis=0)
        mhi, mlo = split(m_ref[t])
        tm = ndot(mhi, cmat) + ndot(mlo, cmat)
        thi, tlo = split(tm)
        gram = tdot(cmat, thi) + tdot(cmat, tlo)
        level = jnp.sum(jnp.where(r == c, gram, 0.0), axis=1, keepdims=True)
        level = jnp.sum(level, axis=0, keepdims=True) / w
        f_ref[t] = gram + jnp.where(r == c, 0.01 * level + 1e-6, 0.0)
        t_ref[t] = tm
    eliminate(f_ref, nt, w)
    root = float(order) ** 0.5
    for t in range(nt):
        fac = f_ref[t]
        diag = jnp.sum(jnp.where(r == c, fac, 0.0), axis=1, keepdims=True)
        linv = (root * lax.rsqrt(diag)) * jnp.where(c < r, fac, jnp.where(c == r, 1.0, 0.0))
        lhi, llo = split(linv)
        cmat = jnp.concatenate([a_ref[t], px_ref[...]], axis=0)
        thi, tlo = split(t_ref[t])
        z = bt(cmat, lhi) + bt(cmat, llo)
        coef = (bt(thi, lhi) + bt(tlo, lhi) + bt(thi, llo)) * (1.0 / order)
        rank = trank[t]
        keep = listed[t] == 1
        coef1 = jnp.where(r < rank, coef[:w], 0.0)
        coef2 = jnp.where(r < crank[0], coef[w:], 0.0)
        eye = jnp.where((r == c) & (r < rank), 1.0, 0.0)
        shift = jnp.where((c == r + rank) & (r < crank[0]), 1.0, 0.0)
        zhi, zlo = split(jnp.concatenate([jnp.where(keep, z[:w], eye), jnp.where(keep, z[w:], shift)], axis=0))
        z_ref[t] = jnp.concatenate([zhi, zlo], axis=1)
        rv = jnp.concatenate([jnp.where(keep, coef1, eye), -jnp.where(keep, coef2, shift)], axis=0)
        rv_ref[t] = rv.astype(bf16)


def back_kernel(u_ref, p_ref, v_ref, x_ref, z_ref, rv_ref, ou_ref, ov_ref):
    w = u_ref.shape[-1]
    up = jnp.concatenate([u_ref[0], p_ref[0]], axis=1)
    both = ndot(up, z_ref[0])
    ou_ref[0] = (both[:, :w] + both[:, w:]).astype(bf16)
    vx = jnp.concatenate([v_ref[0], x_ref[0]], axis=1)
    ov_ref[0] = ndot(vx, rv_ref[0]).astype(bf16)


def local_work(u, v, trank, listed, pan_u, pan_v, rrank, side_u, side_v, crank, sketch):
    nt, order, w = u.shape
    smem = pl.BlockSpec(memory_space=pltpu.SMEM)
    vmem = pl.BlockSpec(memory_space=pltpu.VMEM)
    tile = pl.BlockSpec((1, order, w), lambda i: (i, 0, 0))
    fixed = pl.BlockSpec((1, order, w), lambda i: (0, 0, 0))
    m, a, left, px = pl.pallas_call(
        front_kernel,
        grid=(nt,),
        out_shape=(
            jax.ShapeDtypeStruct((nt, 2 * w, 2 * w), f32),
            jax.ShapeDtypeStruct((nt, w, w), bf16),
            jax.ShapeDtypeStruct((nt, order, w), bf16),
            jax.ShapeDtypeStruct((w, w), bf16),
        ),
        in_specs=[smem, smem, smem, tile, tile, tile, tile, fixed, fixed, pl.BlockSpec((order, w), lambda i: (0, 0))],
        out_specs=(
            pl.BlockSpec((1, 2 * w, 2 * w), lambda i: (i, 0, 0)),
            pl.BlockSpec((1, w, w), lambda i: (i, 0, 0)),
            tile,
            pl.BlockSpec((w, w), lambda i: (0, 0)),
        ),
    )(trank, rrank, crank, pan_v, pan_u, u, v, side_v, side_u, sketch)
    z, rv = pl.pallas_call(
        functools.partial(mid_kernel, order),
        out_shape=(jax.ShapeDtypeStruct((nt, 2 * w, 2 * w), bf16), jax.ShapeDtypeStruct((nt, 2 * w, w), bf16)),
        in_specs=[smem, smem, smem, vmem, vmem, vmem],
        out_specs=(vmem, vmem),
        scratch_shapes=[pltpu.VMEM((nt, w, w), f32), pltpu.VMEM((nt, 2 * w, w), f32)],
    )(trank, crank, listed, m, a, px)
    return pl.pallas_call(
        back_kernel,
        grid=(nt,),
        out_shape=(jax.ShapeDtypeStruct(u.shape, bf16), jax.ShapeDtypeStruct(u.shape, bf16)),
        in_specs=[
            tile,
            tile,
            tile,
            fixed,
            pl.BlockSpec((1, 2 * w, 2 * w), lambda i: (i, 0, 0)),
            pl.BlockSpec((1, 2 * w, w), lambda i: (i, 0, 0)),
        ],
        out_specs=(tile, tile),
    )(u, left, v, side_u, z, rv)


def on_device(
    tile_u, tile_v, tile_rank, listed, row_u, row_v, row_rank, col_u, col_v, col_rank, sketch
):
    rows = tile_u.shape[0]
    both = lax.all_gather(jnp.concatenate([row_u, row_v], axis=0), "col", axis=1, tiled=True)
    pan_u, pan_v = both[:rows], both[rows:]
    side = lax.all_gather(jnp.concatenate([col_u, col_v], axis=0), "row", axis=1, tiled=True)
    side_u, side_v = side[:1], side[1:]
    out_u, out_v = local_work(
        tile_u[:, 0], tile_v[:, 0], tile_rank[:, 0], listed[:, 0], pan_u, pan_v, row_rank, side_u, side_v, col_rank, sketch
    )
    return (out_u[:, None], out_v[:, None])


def solution(mesh):
    return jax.shard_map(
        on_device,
        mesh=mesh,
        in_specs=(
            P("row", "col", None, None),
            P("row", "col", None, None),
            P("row", "col"),
            P("row", "col"),
            P("row", "col", None),
            P("row", "col", None),
            P("row"),
            P("col", "row", None),
            P("col", "row", None),
            P("col"),
            P(),
        ),
        out_specs=(P("row", "col", None, None), P("row", "col", None, None)),
        check_vma=False,
    )
```

```python
import functools

import jax
import jax.numpy as jnp
from jax import lax
from jax.experimental import pallas as pl
from jax.experimental.pallas import tpu as pltpu
from jax.sharding import PartitionSpec as P

f32 = jnp.float32
bf16 = jnp.bfloat16
NB = 32


def tdot(a, b):
    return lax.dot_general(a, b, (((0,), (0,)), ((), ())), preferred_element_type=f32)


def ndot(a, b):
    return lax.dot_general(a, b, (((1,), (0,)), ((), ())), preferred_element_type=f32)


def split(x):
    hi = x.astype(bf16)
    return hi, (x - hi.astype(f32)).astype(bf16)


def iota(shape, dim):
    return lax.broadcasted_iota(jnp.int32, shape, dim)


def ring_stage(blk, half, pos, n, device, sends, recvs):
    right, left = lax.rem(pos + 1, n), lax.rem(pos + n - 1, n)

    far = lax.rem(pos + 2, n)

    def copy(into, k):
        if k < 2:
            ref = blk((left, right)[k] if into else pos)
        else:
            ref = half(far if into else (left, right)[k - 2], k - 2)
        return pltpu.make_async_remote_copy(
            src_ref=ref,
            dst_ref=ref,
            send_sem=sends(k),
            recv_sem=recvs(k),
            device_id=device((right, left)[k % 2]),
            device_id_type=pl.DeviceIdType.MESH,
        )

    return functools.partial(copy, False), functools.partial(copy, True)


def begin(stage):
    stage[0](0).start()
    stage[0](1).start()


def forward(stage):
    stage[1](0).wait_recv()
    stage[0](2).start()
    stage[1](1).wait_recv()
    stage[0](3).start()


def arrived(stage):
    stage[1](2).wait_recv()
    stage[1](3).wait_recv()


def sent(stage):
    for k in range(4):
        stage[0](k).wait_send()


def gather_kernel(
    sizes, trank, rrank, crank, rowu_ref, rowv_ref, colu_ref, colv_ref, u_ref, v_ref, s_ref, m_ref, a_ref, px_ref, left_ref, side_ref,
    qbuf, pbuf, cbuf, ubuf, vbuf, lbuf, local, usem, vsem, lsem, gsend, grecv, csend, crecv, psend, precv
):
    nz, nc, ny, nx = sizes
    nt, w = qbuf.shape[0], u_ref.shape[-1]
    row, col = lax.axis_index("row"), lax.axis_index("col")
    z, core = row // nc, lax.rem(row, nc)
    y, x = col // nx, lax.rem(col, nx)

    def at_x(px):
        return (row, y * nx + px)

    def at_y(py):
        return (row, py * nx + x)

    def at_z(pz):
        return (pz * nc + core, col)

    partner = (z * nc + (1 - core), col)
    near = [at_x(lax.rem(x + 1, nx)), at_x(lax.rem(x + nx - 1, nx)), at_y(lax.rem(y + 1, ny)), at_y(lax.rem(y + ny - 1, ny))]
    near += [at_z(lax.rem(z + 1, nz)), at_z(lax.rem(z + nz - 1, nz)), partner]
    barrier = pltpu.get_barrier_semaphore()
    for device in near:
        pl.semaphore_signal(barrier, inc=1, device_id=device, device_id_type=pl.DeviceIdType.MESH)

    own = [
        pltpu.make_async_copy(colv_ref.at[0], cbuf.at[0, z, core], local.at[0]),
        pltpu.make_async_copy(colu_ref.at[0], cbuf.at[1, z, core], local.at[1]),
        pltpu.make_async_copy(rowv_ref, qbuf.at[:, y, x], local.at[2]),
        pltpu.make_async_copy(rowu_ref, pbuf.at[:, y, x], local.at[3]),
    ]
    for copy in own:
        copy.start()

    def load_u(i):
        return pltpu.make_async_copy(u_ref.at[i], ubuf.at[i], usem.at[i])

    def load_v(i):
        return pltpu.make_async_copy(v_ref.at[i], vbuf.at[i], vsem.at[i])

    def store_left(i):
        return pltpu.make_async_copy(lbuf.at[i], left_ref.at[i], lsem.at[i])

    def for_tiles(body):
        lax.fori_loop(0, nt, lambda i, c: (body(i), c)[1], 0)

    hw, hc = w // 2, cbuf.shape[3] // 2

    def panel(k):
        return ring_stage(
            lambda p: cbuf.at[k, p, core], lambda p, h: cbuf.at[k, p, core, pl.ds(hc * h, hc)], z, nz, at_z,
            lambda c: csend.at[k, c], lambda c: crecv.at[k, c],
        )

    def across(k):
        def copy(into):
            c = 1 - core if into else core
            return pltpu.make_async_remote_copy(
                src_ref=cbuf.at[k, :, c],
                dst_ref=cbuf.at[k, :, c],
                send_sem=psend.at[k],
                recv_sem=precv.at[k],
                device_id=partner,
                device_id_type=pl.DeviceIdType.MESH,
            )

        return functools.partial(copy, False), functools.partial(copy, True)

    def first(i):
        q = ring_stage(
            lambda p: qbuf.at[i, y, p], lambda p, h: qbuf.at[i, y, p, pl.ds(hw * h, hw)], x, nx, at_x,
            lambda c: gsend.at[i, 0, c], lambda c: grecv.at[i, 0, c],
        )
        p = ring_stage(
            lambda p: pbuf.at[i, p, x], lambda p, h: pbuf.at[i, p, x, pl.ds(hw * h, hw)], y, ny, at_y,
            lambda c: gsend.at[i, 1, c], lambda c: grecv.at[i, 1, c],
        )
        return q, p

    def second(i):
        q = ring_stage(
            lambda p: qbuf.at[i, p], lambda p, h: qbuf.at[i, p, pl.ds(nx // 2 * h, nx // 2)], y, ny, at_y,
            lambda c: gsend.at[i, 2, c], lambda c: grecv.at[i, 2, c],
        )
        p = ring_stage(
            lambda p: pbuf.at[i, :, p], lambda p, h: pbuf.at[i, pl.ds(ny // 2 * h, ny // 2), p], x, nx, at_x,
            lambda c: gsend.at[i, 3, c], lambda c: grecv.at[i, 3, c],
        )
        return q, p

    def each(stages, act):
        for stage in stages:
            act(stage)

    def enter_second(i):
        each(first(i), arrived)
        each(second(i), begin)

    for copy in own:
        copy.wait()
    pl.semaphore_wait(barrier, len(near))
    begin(panel(0))
    begin(panel(1))
    for_tiles(lambda i: each(first(i), begin))
    for_tiles(lambda i: load_v(i).start())
    for_tiles(lambda i: load_u(i).start())
    each(first(0), forward)
    forward(panel(0))
    each(first(1), forward)
    forward(panel(1))
    enter_second(0)
    for k in range(2):
        arrived(panel(k))
        across(k)[0]().start()
    enter_second(1)
    each(first(2), forward)
    each(second(0), forward)

    r, c = iota((w, w), 0), iota((w, w), 1)
    for k in range(2):
        across(k)[1]().wait_recv()
    order = u_ref.shape[1]
    xs = cbuf[1].reshape(order, w)
    side_ref[0] = xs
    px_ref[...] = jnp.where(r < crank[0], -tdot(xs, s_ref[...]), 0.0).astype(bf16)
    each(second(0), arrived)

    def math(i):
        core_ij = tdot(qbuf[i].reshape(order, w), cbuf[0].reshape(order, w))
        core_ij = jnp.where((r < rrank[i]) & (c < crank[0]), core_ij, 0.0).astype(bf16)
        load_v(i).wait()
        proj = tdot(vbuf[i], s_ref[...])
        a_ref[i] = jnp.where(r < trank[i], proj, 0.0).astype(bf16)
        left = ndot(pbuf[i].reshape(order, w), core_ij).astype(bf16)
        lbuf[i] = left
        load_u(i).wait()
        both = jnp.concatenate([ubuf[i], left], axis=1)
        m_ref[i] = tdot(both, both)
        store_left(i).start()

    @pl.loop(1, nt)
    def _(i):
        @pl.when(i + 1 < nt)
        def _():
            enter_second(i + 1)

        @pl.when(i + 2 < nt)
        def _():
            each(first(i + 2), forward)

        each(second(i), forward)
        math(i - 1)
        each(second(i), arrived)

    math(nt - 1)
    for k in range(2):
        sent(panel(k))
        across(k)[0]().wait_send()
    for_tiles(lambda i: (each(first(i), sent), each(second(i), sent)))
    for_tiles(lambda i: store_left(i).wait())


def eliminate(f_ref, nt, w):
    lane3 = iota((1, 1, w), 2)
    sub3 = iota((1, 8, 1), 1)
    lane2, row2 = iota((NB, w), 1), iota((NB, w), 0)
    for p in range(w // NB):
        r0 = NB * p
        parts = [f_ref[:, r0 + 8 * q : r0 + 8 * q + 8, :] for q in range(NB // 8)]
        for k in range(NB):
            c, q0, s = r0 + k, k // 8, k % 8
            cols = [jnp.broadcast_to(parts[q][:, :, c : c + 1], (nt, 8, w)) for q in range(q0, NB // 8)]
            inv = 1.0 / cols[0][:, s : s + 1, :]
            row = parts[q0][:, s : s + 1, :]
            row = jnp.where(lane3 == c, 1.0, row) * inv
            for q in range(q0, NB // 8):
                col, here = cols[q - q0], lane3 == c
                if q == q0:
                    col = jnp.where(sub3 > s, col, 0.0)
                    here = here & (sub3 > s)
                parts[q] = jnp.where(here, 0.0, parts[q]) - col * row
        for q in range(NB // 8):
            f_ref[:, r0 + 8 * q : r0 + 8 * q + 8, :] = parts[q]
        if r0 + NB < w:
            for t in range(nt):
                panel = f_ref[t, r0 : r0 + NB, :]
                diag = jnp.sum(jnp.where(lane2 == row2 + r0, panel, 0.0), axis=1, keepdims=True)
                mult = panel * (1.0 / diag)
                inside = (lane2 >= r0) & (lane2 < r0 + NB)
                unit = jnp.where(lane2 - r0 < row2, panel, jnp.where(lane2 - r0 == row2, 1.0, 0.0))
                rhs = jnp.where(inside, unit, panel)
                upd = lax.dot_general(
                    mult, rhs, (((0,), (0,)), ((), ())), preferred_element_type=f32, precision=lax.Precision.HIGHEST
                )[r0 + NB :, :]
                old = f_ref[t, r0 + NB :, :]
                lane = iota(old.shape, 1)
                old = jnp.where((lane >= r0) & (lane < r0 + NB), 0.0, old)
                f_ref[t, r0 + NB :, :] = old - upd


def bt(a, b):
    return lax.dot_general(a, b, (((1,), (1,)), ((), ())), preferred_element_type=f32)


def mid_kernel(order, trank, crank, listed, m_ref, a_ref, px_ref, z_ref, rv_ref, f_ref, t_ref):
    nt, w = a_ref.shape[0], a_ref.shape[-1]
    r, c = iota((w, w), 0), iota((w, w), 1)
    for t in range(nt):
        cmat = jnp.concatenate([a_ref[t], px_ref[...]], axis=0)
        mhi, mlo = split(m_ref[t])
        tm = ndot(mhi, cmat) + ndot(mlo, cmat)
        thi, tlo = split(tm)
        gram = tdot(cmat, thi) + tdot(cmat, tlo)
        level = jnp.sum(jnp.where(r == c, gram, 0.0), axis=1, keepdims=True)
        level = jnp.sum(level, axis=0, keepdims=True) / w
        f_ref[t] = gram + jnp.where(r == c, 0.01 * level + 1e-6, 0.0)
        t_ref[t] = tm
    eliminate(f_ref, nt, w)
    root = float(order) ** 0.5
    for t in range(nt):
        fac = f_ref[t]
        diag = jnp.sum(jnp.where(r == c, fac, 0.0), axis=1, keepdims=True)
        linv = (root * lax.rsqrt(diag)) * jnp.where(c < r, fac, jnp.where(c == r, 1.0, 0.0))
        lhi, llo = split(linv)
        cmat = jnp.concatenate([a_ref[t], px_ref[...]], axis=0)
        thi, tlo = split(t_ref[t])
        z = bt(cmat, lhi) + bt(cmat, llo)
        coef = (bt(thi, lhi) + bt(tlo, lhi) + bt(thi, llo)) * (1.0 / order)
        rank = trank[t]
        keep = listed[t] == 1
        coef1 = jnp.where(r < rank, coef[:w], 0.0)
        coef2 = jnp.where(r < crank[0], coef[w:], 0.0)
        eye = jnp.where((r == c) & (r < rank), 1.0, 0.0)
        shift = jnp.where((c == r + rank) & (r < crank[0]), 1.0, 0.0)
        zhi, zlo = split(jnp.concatenate([jnp.where(keep, z[:w], eye), jnp.where(keep, z[w:], shift)], axis=0))
        z_ref[t] = jnp.concatenate([zhi, zlo], axis=1)
        rv = jnp.concatenate([jnp.where(keep, coef1, eye), -jnp.where(keep, coef2, shift)], axis=0)
        rv_ref[t] = rv.astype(bf16)


def back_kernel(u_ref, p_ref, v_ref, x_ref, z_ref, rv_ref, ou_ref, ov_ref):
    w = u_ref.shape[-1]
    up = jnp.concatenate([u_ref[0], p_ref[0]], axis=1)
    both = ndot(up, z_ref[0])
    ou_ref[0] = (both[:, :w] + both[:, w:]).astype(bf16)
    vx = jnp.concatenate([v_ref[0], x_ref[0]], axis=1)
    ov_ref[0] = ndot(vx, rv_ref[0]).astype(bf16)


def front(mesh_sizes, u, v, trank, row_u, row_v, rrank, col_u, col_v, crank, sketch):
    nt, order, w = u.shape
    nz, nc, ny, nx = mesh_sizes
    smem = pl.BlockSpec(memory_space=pltpu.SMEM)
    vmem = pl.BlockSpec(memory_space=pltpu.VMEM)
    hbm = pl.BlockSpec(memory_space=pl.ANY)
    dma = pltpu.SemaphoreType.DMA
    return pl.pallas_call(
        functools.partial(gather_kernel, mesh_sizes),
        out_shape=(
            jax.ShapeDtypeStruct((nt, 2 * w, 2 * w), f32),
            jax.ShapeDtypeStruct((nt, w, w), bf16),
            jax.ShapeDtypeStruct((w, w), bf16),
            jax.ShapeDtypeStruct((nt, order, w), bf16),
            jax.ShapeDtypeStruct((1, order, w), bf16),
        ),
        in_specs=[smem, smem, smem, hbm, hbm, hbm, hbm, hbm, hbm, vmem],
        out_specs=(vmem, vmem, vmem, hbm, vmem),
        scratch_shapes=[
            pltpu.VMEM((nt, ny, nx, w, w), bf16),
            pltpu.VMEM((nt, ny, nx, w, w), bf16),
            pltpu.VMEM((2, nz, nc, order // (nz * nc), w), bf16),
            pltpu.VMEM((nt, order, w), bf16),
            pltpu.VMEM((nt, order, w), bf16),
            pltpu.VMEM((nt, order, w), bf16),
            dma((4,)),
            dma((nt,)),
            dma((nt,)),
            dma((nt,)),
            dma((nt, 4, 4)),
            dma((nt, 4, 4)),
            dma((2, 4)),
            dma((2, 4)),
            dma((2,)),
            dma((2,)),
        ],
        compiler_params=pltpu.CompilerParams(collective_id=0, has_side_effects=True, vmem_limit_bytes=48 * 1024 * 1024),
    )(trank, rrank, crank, row_u, row_v, col_u, col_v, u, v, sketch)


def local_work(u, v, trank, listed, m, a, px, left, side_u, crank):
    nt, order, w = u.shape
    smem = pl.BlockSpec(memory_space=pltpu.SMEM)
    vmem = pl.BlockSpec(memory_space=pltpu.VMEM)
    tile = pl.BlockSpec((1, order, w), lambda i: (i, 0, 0))
    fixed = pl.BlockSpec((1, order, w), lambda i: (0, 0, 0))
    z, rv = pl.pallas_call(
        functools.partial(mid_kernel, order),
        out_shape=(jax.ShapeDtypeStruct((nt, 2 * w, 2 * w), bf16), jax.ShapeDtypeStruct((nt, 2 * w, w), bf16)),
        in_specs=[smem, smem, smem, vmem, vmem, vmem],
        out_specs=(vmem, vmem),
        scratch_shapes=[pltpu.VMEM((nt, w, w), f32), pltpu.VMEM((nt, 2 * w, w), f32)],
    )(trank, crank, listed, m, a, px)
    return pl.pallas_call(
        back_kernel,
        grid=(nt,),
        out_shape=(jax.ShapeDtypeStruct(u.shape, bf16), jax.ShapeDtypeStruct(u.shape, bf16)),
        in_specs=[
            tile,
            tile,
            tile,
            fixed,
            pl.BlockSpec((1, 2 * w, 2 * w), lambda i: (i, 0, 0)),
            pl.BlockSpec((1, 2 * w, w), lambda i: (i, 0, 0)),
        ],
        out_specs=(tile, tile),
    )(u, left, v, side_u, z, rv)


def on_device(
    sizes, tile_u, tile_v, tile_rank, listed, row_u, row_v, row_rank, col_u, col_v, col_rank, sketch
):
    u, v, trank = tile_u[:, 0], tile_v[:, 0], tile_rank[:, 0]
    m, a, px, left, side_u = front(sizes, u, v, trank, row_u, row_v, row_rank, col_u, col_v, col_rank, sketch)
    out_u, out_v = local_work(u, v, trank, listed[:, 0], m, a, px, left, side_u, col_rank)
    return (out_u[:, None], out_v[:, None])


def solution(mesh):
    return jax.shard_map(
        functools.partial(on_device, (mesh.shape["row"] // 2, 2, 4, mesh.shape["col"] // 4)),
        mesh=mesh,
        in_specs=(
            P("row", "col", None, None),
            P("row", "col", None, None),
            P("row", "col"),
            P("row", "col"),
            P("row", "col", None),
            P("row", "col", None),
            P("row"),
            P("col", "row", None),
            P("col", "row", None),
            P("col"),
            P(),
        ),
        out_specs=(P("row", "col", None, None), P("row", "col", None, None)),
        check_vma=False,
    )
```

```python
import functools

import jax
import jax.numpy as jnp
from jax import lax
from jax.experimental import pallas as pl
from jax.experimental.pallas import tpu as pltpu
from jax.sharding import PartitionSpec as P

f32 = jnp.float32
bf16 = jnp.bfloat16
NB = 32


def tdot(a, b):
    return lax.dot_general(a, b, (((0,), (0,)), ((), ())), preferred_element_type=f32)


def ndot(a, b):
    return lax.dot_general(a, b, (((1,), (0,)), ((), ())), preferred_element_type=f32)


def split(x):
    hi = x.astype(bf16)
    return hi, (x - hi.astype(f32)).astype(bf16)


def iota(shape, dim):
    return lax.broadcasted_iota(jnp.int32, shape, dim)


def ring_stage(blk, half, pos, n, device, sends, recvs):
    right, left = lax.rem(pos + 1, n), lax.rem(pos + n - 1, n)

    far = lax.rem(pos + 2, n)

    def copy(into, k):
        if k < 2:
            ref = blk((left, right)[k] if into else pos)
        else:
            ref = half(far if into else (left, right)[k - 2], k - 2)
        return pltpu.make_async_remote_copy(
            src_ref=ref,
            dst_ref=ref,
            send_sem=sends(k),
            recv_sem=recvs(k),
            device_id=device((right, left)[k % 2]),
            device_id_type=pl.DeviceIdType.MESH,
        )

    return functools.partial(copy, False), functools.partial(copy, True)


def begin(stage):
    stage[0](0).start()
    stage[0](1).start()


def forward(stage):
    stage[1](0).wait_recv()
    stage[0](2).start()
    stage[1](1).wait_recv()
    stage[0](3).start()


def arrived(stage):
    stage[1](2).wait_recv()
    stage[1](3).wait_recv()


def sent(stage):
    for k in range(4):
        stage[0](k).wait_send()


def gather_kernel(
    sizes, trank, rrank, crank, rowu_ref, rowv_ref, colu_ref, colv_ref, u_ref, v_ref, s_ref, m_ref, a_ref, px_ref, left_ref, side_ref,
    qbuf, pbuf, cbuf, ubuf, vbuf, lbuf, local, usem, vsem, lsem, gsend, grecv, csend, crecv, psend, precv
):
    nz, nc, ny, nx = sizes
    ng, g, w = qbuf.shape[0], qbuf.shape[3], u_ref.shape[-1]
    nt = ng * g
    row, col = lax.axis_index("row"), lax.axis_index("col")
    z, core = row // nc, lax.rem(row, nc)
    y, x = col // nx, lax.rem(col, nx)

    def at_x(px):
        return (row, y * nx + px)

    def at_y(py):
        return (row, py * nx + x)

    def at_z(pz):
        return (pz * nc + core, col)

    partner = (z * nc + (1 - core), col)
    near = [at_x(lax.rem(x + 1, nx)), at_x(lax.rem(x + nx - 1, nx)), at_y(lax.rem(y + 1, ny)), at_y(lax.rem(y + ny - 1, ny))]
    near += [at_z(lax.rem(z + 1, nz)), at_z(lax.rem(z + nz - 1, nz)), partner]
    barrier = pltpu.get_barrier_semaphore()
    for device in near:
        pl.semaphore_signal(barrier, inc=1, device_id=device, device_id_type=pl.DeviceIdType.MESH)

    own = [
        pltpu.make_async_copy(colv_ref.at[0], cbuf.at[0, z, core], local.at[0]),
        pltpu.make_async_copy(colu_ref.at[0], cbuf.at[1, z, core], local.at[1]),
        pltpu.make_async_copy(rowv_ref, qbuf.at[:, y, x], local.at[2]),
        pltpu.make_async_copy(rowu_ref, pbuf.at[:, y, x], local.at[3]),
    ]
    for copy in own:
        copy.start()

    def load_u(i):
        return pltpu.make_async_copy(u_ref.at[i], ubuf.at[i], usem.at[i])

    def load_v(i):
        return pltpu.make_async_copy(v_ref.at[i], vbuf.at[i], vsem.at[i])

    def store_left(i):
        return pltpu.make_async_copy(lbuf.at[i], left_ref.at[i], lsem.at[i])

    def for_tiles(body):
        lax.fori_loop(0, nt, lambda i, c: (body(i), c)[1], 0)

    def for_groups(body):
        lax.fori_loop(0, ng, lambda i, c: (body(i), c)[1], 0)

    hw, hc = g // 2, cbuf.shape[3] // 2

    def panel(k):
        return ring_stage(
            lambda p: cbuf.at[k, p, core], lambda p, h: cbuf.at[k, p, core, pl.ds(hc * h, hc)], z, nz, at_z,
            lambda c: csend.at[k, c], lambda c: crecv.at[k, c],
        )

    def across(k):
        def copy(into):
            c = 1 - core if into else core
            return pltpu.make_async_remote_copy(
                src_ref=cbuf.at[k, :, c],
                dst_ref=cbuf.at[k, :, c],
                send_sem=psend.at[k],
                recv_sem=precv.at[k],
                device_id=partner,
                device_id_type=pl.DeviceIdType.MESH,
            )

        return functools.partial(copy, False), functools.partial(copy, True)

    def first(i):
        q = ring_stage(
            lambda p: qbuf.at[i, y, p], lambda p, h: qbuf.at[i, y, p, pl.ds(hw * h, hw)], x, nx, at_x,
            lambda c: gsend.at[i, 0, c], lambda c: grecv.at[i, 0, c],
        )
        p = ring_stage(
            lambda p: pbuf.at[i, p, x], lambda p, h: pbuf.at[i, p, x, pl.ds(hw * h, hw)], y, ny, at_y,
            lambda c: gsend.at[i, 1, c], lambda c: grecv.at[i, 1, c],
        )
        return q, p

    def second(i):
        q = ring_stage(
            lambda p: qbuf.at[i, p], lambda p, h: qbuf.at[i, p, pl.ds(nx // 2 * h, nx // 2)], y, ny, at_y,
            lambda c: gsend.at[i, 2, c], lambda c: grecv.at[i, 2, c],
        )
        p = ring_stage(
            lambda p: pbuf.at[i, :, p], lambda p, h: pbuf.at[i, pl.ds(ny // 2 * h, ny // 2), p], x, nx, at_x,
            lambda c: gsend.at[i, 3, c], lambda c: grecv.at[i, 3, c],
        )
        return q, p

    def each(stages, act):
        for stage in stages:
            act(stage)

    def enter_second(i):
        each(first(i), arrived)
        each(second(i), begin)

    for copy in own:
        copy.wait()
    pl.semaphore_wait(barrier, len(near))
    begin(panel(0))
    begin(panel(1))
    for_groups(lambda i: each(first(i), begin))
    for_tiles(lambda i: load_v(i).start())
    for_tiles(lambda i: load_u(i).start())
    each(first(0), forward)
    forward(panel(0))
    enter_second(0)
    each(first(1), forward)
    forward(panel(1))
    for k in range(2):
        arrived(panel(k))
        across(k)[0]().start()
    enter_second(1)
    each(first(2), forward)
    each(second(0), forward)

    r, c = iota((w, w), 0), iota((w, w), 1)
    for k in range(2):
        across(k)[1]().wait_recv()
    order = u_ref.shape[1]
    xs = cbuf[1].reshape(order, w)
    side_ref[0] = xs
    px_ref[...] = jnp.where(r < crank[0], -tdot(xs, s_ref[...]), 0.0).astype(bf16)
    each(second(0), arrived)

    def math(n, k):
        i = n * g + k
        core_ij = tdot(qbuf[n, :, :, k].reshape(order, w), cbuf[0].reshape(order, w))
        core_ij = jnp.where((r < rrank[i]) & (c < crank[0]), core_ij, 0.0).astype(bf16)
        load_v(i).wait()
        proj = tdot(vbuf[i], s_ref[...])
        a_ref[i] = jnp.where(r < trank[i], proj, 0.0).astype(bf16)
        left = ndot(pbuf[n, :, :, k].reshape(order, w), core_ij).astype(bf16)
        lbuf[i] = left
        load_u(i).wait()
        both = jnp.concatenate([ubuf[i], left], axis=1)
        m_ref[i] = tdot(both, both)
        store_left(i).start()

    @pl.loop(1, ng)
    def _(n):
        @pl.when(n + 1 < ng)
        def _():
            enter_second(n + 1)

        @pl.when(n + 2 < ng)
        def _():
            each(first(n + 2), forward)

        math(n - 1, 0)
        each(second(n), forward)
        for k in range(1, g):
            math(n - 1, k)
        each(second(n), arrived)

    for k in range(g):
        math(ng - 1, k)
    for k in range(2):
        sent(panel(k))
        across(k)[0]().wait_send()
    for_groups(lambda i: (each(first(i), sent), each(second(i), sent)))
    for_tiles(lambda i: store_left(i).wait())


def eliminate_block(parts, q0, base, nt, w):
    lane, sub, n = iota((1, 1, w), 2), iota((1, 8, 1), 1), len(parts)
    cols = {q: [jnp.broadcast_to(parts[q][:, :, base + c : base + c + 1], (nt, 8, w)) for c in range(8)] for q in range(q0, n)}
    head = cols[q0]
    for i in range(0, 8, 2):
        j = i + 1
        on_i, on_j = lane == base + i, lane == base + j
        a, b, d = head[i][:, i:j], head[j][:, i:j], head[j][:, j : j + 1]
        inv_i = 1.0 / a
        inv_j = a * (1.0 / (a * d - b * b))
        ratio = b * inv_i
        row_i = jnp.where(on_i, 1.0, parts[q0][:, i:j]) * inv_i
        new_j = jnp.where(on_i, 0.0, parts[q0][:, j : j + 1]) - b * row_i
        row_j = jnp.where(on_j, 1.0, new_j) * inv_j
        row_i = jnp.where(on_j, 0.0, row_i)
        to_i = {c: head[c][:, i:j] * inv_i for c in range(j + 1, 8)}
        to_j = {c: (head[c][:, j : j + 1] - b * to_i[c]) * inv_j for c in range(j + 1, 8)}
        for q in range(q0, n):
            mul_i, mul_j = cols[q][i], cols[q][j] - cols[q][i] * ratio
            clear = on_i | on_j
            if q == q0:
                clear = clear & (sub > j)
                mul_i, mul_j = jnp.where(sub > j, mul_i, 0.0), jnp.where(sub > j, mul_j, 0.0)
            rows = jnp.where(clear, 0.0, parts[q]) - mul_i * row_i - mul_j * row_j
            parts[q] = jnp.where(sub == j, new_j, rows) if q == q0 else rows
            for c in range(j + 1, 8):
                cols[q][c] = cols[q][c] - mul_i * to_i[c] - mul_j * to_j[c]


def eliminate(f_ref, t0, nt, w, between=lambda: None):
    lane2, row2 = iota((NB, w), 1), iota((NB, w), 0)
    for r0 in range(0, w, NB):
        spots = [(pl.ds(t0, nt), pl.ds(r0 + 8 * q, 8)) for q in range(NB // 8)]
        parts = [f_ref[spot] for spot in spots]
        for q0 in range(NB // 8):
            eliminate_block(parts, q0, r0 + 8 * q0, nt, w)
            between()
        for spot, part in zip(spots, parts):
            f_ref[spot] = part
        if r0 + NB == w:
            break
        inside = (lane2 >= r0) & (lane2 < r0 + NB)
        for t in range(t0, t0 + nt):
            panel = f_ref[t, r0 : r0 + NB, :]
            diag = jnp.sum(jnp.where(lane2 == row2 + r0, panel, 0.0), axis=1, keepdims=True)
            unit = jnp.where(lane2 - r0 < row2, panel, jnp.where(lane2 - r0 == row2, 1.0, 0.0))
            upd = lax.dot_general(
                panel * (1.0 / diag), jnp.where(inside, unit, panel), (((0,), (0,)), ((), ())),
                preferred_element_type=f32, precision=lax.Precision.HIGHEST,
            )[r0 + NB :, :]
            old = f_ref[t, r0 + NB :, :]
            lane = iota(old.shape, 1)
            f_ref[t, r0 + NB :, :] = jnp.where((lane >= r0) & (lane < r0 + NB), 0.0, old) - upd


def bt(a, b):
    return lax.dot_general(a, b, (((1,), (1,)), ((), ())), preferred_element_type=f32)


def mid_kernel(order, trank, crank, listed, m_ref, a_ref, px_ref, z_ref, rv_ref, f_ref, t_ref):
    nt, w = a_ref.shape[0], a_ref.shape[-1]
    r, c = iota((w, w), 0), iota((w, w), 1)
    for t in range(nt):
        cmat = jnp.concatenate([a_ref[t], px_ref[...]], axis=0)
        mhi, mlo = split(m_ref[t])
        tm = ndot(mhi, cmat) + ndot(mlo, cmat)
        thi, tlo = split(tm)
        gram = tdot(cmat, thi) + tdot(cmat, tlo)
        level = jnp.sum(jnp.where(r == c, gram, 0.0), axis=1, keepdims=True)
        level = jnp.sum(level, axis=0, keepdims=True) / w
        f_ref[t] = gram + jnp.where(r == c, 0.01 * level + 1e-6, 0.0)
        t_ref[t] = tm
    eliminate(f_ref, 0, nt, w)
    root = float(order) ** 0.5
    for t in range(nt):
        fac = f_ref[t]
        diag = jnp.sum(jnp.where(r == c, fac, 0.0), axis=1, keepdims=True)
        linv = (root * lax.rsqrt(diag)) * jnp.where(c < r, fac, jnp.where(c == r, 1.0, 0.0))
        lhi, llo = split(linv)
        cmat = jnp.concatenate([a_ref[t], px_ref[...]], axis=0)
        thi, tlo = split(t_ref[t])
        z = bt(cmat, lhi) + bt(cmat, llo)
        coef = (bt(thi, lhi) + bt(tlo, lhi) + bt(thi, llo)) * (1.0 / order)
        rank = trank[t]
        keep = listed[t] == 1
        coef1 = jnp.where(r < rank, coef[:w], 0.0)
        coef2 = jnp.where(r < crank[0], coef[w:], 0.0)
        eye = jnp.where((r == c) & (r < rank), 1.0, 0.0)
        shift = jnp.where((c == r + rank) & (r < crank[0]), 1.0, 0.0)
        zhi, zlo = split(jnp.concatenate([jnp.where(keep, z[:w], eye), jnp.where(keep, z[w:], shift)], axis=0))
        z_ref[t] = jnp.concatenate([zhi, zlo], axis=1)
        rv = jnp.concatenate([jnp.where(keep, coef1, eye), -jnp.where(keep, coef2, shift)], axis=0)
        rv_ref[t] = rv.astype(bf16)


def back_kernel(u_ref, p_ref, v_ref, x_ref, z_ref, rv_ref, ou_ref, ov_ref):
    w = u_ref.shape[-1]
    up = jnp.concatenate([u_ref[0], p_ref[0]], axis=1)
    both = ndot(up, z_ref[0])
    ou_ref[0] = (both[:, :w] + both[:, w:]).astype(bf16)
    vx = jnp.concatenate([v_ref[0], x_ref[0]], axis=1)
    ov_ref[0] = ndot(vx, rv_ref[0]).astype(bf16)


def front(mesh_sizes, u, v, trank, row_u, row_v, rrank, col_u, col_v, crank, sketch):
    nt, order, w = u.shape
    nz, nc, ny, nx = mesh_sizes
    g = 2
    ng = nt // g
    row_u, row_v = (a.reshape(ng, g, *a.shape[1:]) for a in (row_u, row_v))
    smem = pl.BlockSpec(memory_space=pltpu.SMEM)
    vmem = pl.BlockSpec(memory_space=pltpu.VMEM)
    hbm = pl.BlockSpec(memory_space=pl.ANY)
    dma = pltpu.SemaphoreType.DMA
    return pl.pallas_call(
        functools.partial(gather_kernel, mesh_sizes),
        out_shape=(
            jax.ShapeDtypeStruct((nt, 2 * w, 2 * w), f32),
            jax.ShapeDtypeStruct((nt, w, w), bf16),
            jax.ShapeDtypeStruct((w, w), bf16),
            jax.ShapeDtypeStruct((nt, order, w), bf16),
            jax.ShapeDtypeStruct((1, order, w), bf16),
        ),
        in_specs=[smem, smem, smem, hbm, hbm, hbm, hbm, hbm, hbm, vmem],
        out_specs=(vmem, vmem, vmem, hbm, vmem),
        scratch_shapes=[
            pltpu.VMEM((ng, ny, nx, g, w, w), bf16),
            pltpu.VMEM((ng, ny, nx, g, w, w), bf16),
            pltpu.VMEM((2, nz, nc, order // (nz * nc), w), bf16),
            pltpu.VMEM((nt, order, w), bf16),
            pltpu.VMEM((nt, order, w), bf16),
            pltpu.VMEM((nt, order, w), bf16),
            dma((4,)),
            dma((nt,)),
            dma((nt,)),
            dma((nt,)),
            dma((ng, 4, 4)),
            dma((ng, 4, 4)),
            dma((2, 4)),
            dma((2, 4)),
            dma((2,)),
            dma((2,)),
        ],
        compiler_params=pltpu.CompilerParams(collective_id=0, has_side_effects=True, vmem_limit_bytes=62 * 1024 * 1024),
    )(trank, rrank, crank, row_u, row_v, col_u, col_v, u, v, sketch)


def local_work(u, v, trank, listed, m, a, px, left, side_u, crank):
    nt, order, w = u.shape
    smem = pl.BlockSpec(memory_space=pltpu.SMEM)
    vmem = pl.BlockSpec(memory_space=pltpu.VMEM)
    tile = pl.BlockSpec((1, order, w), lambda i: (i, 0, 0))
    fixed = pl.BlockSpec((1, order, w), lambda i: (0, 0, 0))
    z, rv = pl.pallas_call(
        functools.partial(mid_kernel, order),
        out_shape=(jax.ShapeDtypeStruct((nt, 2 * w, 2 * w), bf16), jax.ShapeDtypeStruct((nt, 2 * w, w), bf16)),
        in_specs=[smem, smem, smem, vmem, vmem, vmem],
        out_specs=(vmem, vmem),
        scratch_shapes=[pltpu.VMEM((nt, w, w), f32), pltpu.VMEM((nt, 2 * w, w), f32)],
    )(trank, crank, listed, m, a, px)
    return pl.pallas_call(
        back_kernel,
        grid=(nt,),
        out_shape=(jax.ShapeDtypeStruct(u.shape, bf16), jax.ShapeDtypeStruct(u.shape, bf16)),
        in_specs=[
            tile,
            tile,
            tile,
            fixed,
            pl.BlockSpec((1, 2 * w, 2 * w), lambda i: (i, 0, 0)),
            pl.BlockSpec((1, 2 * w, w), lambda i: (i, 0, 0)),
        ],
        out_specs=(tile, tile),
    )(u, left, v, side_u, z, rv)


def on_device(
    sizes, tile_u, tile_v, tile_rank, listed, row_u, row_v, row_rank, col_u, col_v, col_rank, sketch
):
    u, v, trank = tile_u[:, 0], tile_v[:, 0], tile_rank[:, 0]
    m, a, px, left, side_u = front(sizes, u, v, trank, row_u, row_v, row_rank, col_u, col_v, col_rank, sketch)
    out_u, out_v = local_work(u, v, trank, listed[:, 0], m, a, px, left, side_u, col_rank)
    return (out_u[:, None], out_v[:, None])


def solution(mesh):
    return jax.shard_map(
        functools.partial(on_device, (mesh.shape["row"] // 2, 2, 4, mesh.shape["col"] // 4)),
        mesh=mesh,
        in_specs=(
            P("row", "col", None, None),
            P("row", "col", None, None),
            P("row", "col"),
            P("row", "col"),
            P("row", "col", None),
            P("row", "col", None),
            P("row"),
            P("col", "row", None),
            P("col", "row", None),
            P("col"),
            P(),
        ),
        out_specs=(P("row", "col", None, None), P("row", "col", None, None)),
        check_vma=False,
    )
```

```python
import functools

import jax
import jax.numpy as jnp
from jax import lax
from jax.experimental import pallas as pl
from jax.experimental.pallas import tpu as pltpu
from jax.sharding import PartitionSpec as P

f32 = jnp.float32
bf16 = jnp.bfloat16
NB = 32
PIECES = 4


def tdot(a, b):
    return lax.dot_general(a, b, (((0,), (0,)), ((), ())), preferred_element_type=f32)


def ndot(a, b):
    return lax.dot_general(a, b, (((1,), (0,)), ((), ())), preferred_element_type=f32)


def split(x):
    hi = x.astype(bf16)
    return hi, (x - hi.astype(f32)).astype(bf16)


def iota(shape, dim):
    return lax.broadcasted_iota(jnp.int32, shape, dim)


def ring_stage(blk, half, pos, n, device, sends, recvs):
    right, left = lax.rem(pos + 1, n), lax.rem(pos + n - 1, n)

    far = lax.rem(pos + 2, n)

    def copy(into, k):
        if k < 2:
            ref = blk((left, right)[k] if into else pos)
        else:
            ref = half(far if into else (left, right)[k - 2], k - 2)
        return pltpu.make_async_remote_copy(
            src_ref=ref,
            dst_ref=ref,
            send_sem=sends(k),
            recv_sem=recvs(k),
            device_id=device((right, left)[k % 2]),
            device_id_type=pl.DeviceIdType.MESH,
        )

    return functools.partial(copy, False), functools.partial(copy, True)


def begin(stage):
    stage[0](0).start()
    stage[0](1).start()


def forward(stage):
    stage[1](0).wait_recv()
    stage[0](2).start()
    stage[1](1).wait_recv()
    stage[0](3).start()


def arrived(stage):
    stage[1](2).wait_recv()
    stage[1](3).wait_recv()


def sent(stage):
    for k in range(4):
        stage[0](k).wait_send()


def gather_kernel(
    sizes, trank, rrank, crank, listed, rowu_ref, rowv_ref, colu_ref, colv_ref, u_ref, v_ref, s_ref, m_ref, a_ref, px_ref, left_ref, side_ref, z_ref, rv_ref,
    qbuf, pbuf, cbuf, ubuf, vbuf, lbuf, mbuf, f_ref, t_ref, local, usem, vsem, lsem, fsend, frecv, gsend, grecv, csend, crecv, psend, precv
):
    nz, nc, ny, nx = sizes
    ng, g, w = qbuf.shape[0], qbuf.shape[3], u_ref.shape[-1]
    nt = ng * g
    done = z_ref.shape[0]
    row, col = lax.axis_index("row"), lax.axis_index("col")
    z, core = row // nc, lax.rem(row, nc)
    y, x = col // nx, lax.rem(col, nx)

    def at_x(px):
        return (row, y * nx + px)

    def at_y(py):
        return (row, py * nx + x)

    def at_z(pz):
        return (pz * nc + core, col)

    partner = (z * nc + (1 - core), col)
    near = [at_x(lax.rem(x + 1, nx)), at_x(lax.rem(x + nx - 1, nx)), at_y(lax.rem(y + 1, ny)), at_y(lax.rem(y + ny - 1, ny))]
    near += [at_z(lax.rem(z + 1, nz)), at_z(lax.rem(z + nz - 1, nz)), partner]
    barrier = pltpu.get_barrier_semaphore()
    for device in near:
        pl.semaphore_signal(barrier, inc=1, device_id=device, device_id_type=pl.DeviceIdType.MESH)

    own = [
        pltpu.make_async_copy(colv_ref.at[0], cbuf.at[0, z, core], local.at[0]),
        pltpu.make_async_copy(colu_ref.at[0], cbuf.at[1, z, core], local.at[1]),
        pltpu.make_async_copy(rowv_ref, qbuf.at[:, y, x], local.at[2]),
        pltpu.make_async_copy(rowu_ref, pbuf.at[:, y, x], local.at[3]),
    ]
    for copy in own:
        copy.start()

    def load_u(i):
        return pltpu.make_async_copy(u_ref.at[i], ubuf.at[i], usem.at[i])

    def load_v(i):
        return pltpu.make_async_copy(v_ref.at[i], vbuf.at[i], vsem.at[i])

    def store_left(i):
        return pltpu.make_async_copy(lbuf.at[i], left_ref.at[i], lsem.at[i])

    def for_tiles(body):
        lax.fori_loop(0, nt, lambda i, c: (body(i), c)[1], 0)

    def for_groups(h, body):
        lax.fori_loop(ng // 2 * h, ng // 2 * (h + 1), lambda i, c: (body(i), c)[1], 0)

    hc = cbuf.shape[3] // 2

    def panel(k):
        return ring_stage(
            lambda p: cbuf.at[k, p, core], lambda p, h: cbuf.at[k, p, core, pl.ds(hc * h, hc)], z, nz, at_z,
            lambda c: csend.at[k, c], lambda c: crecv.at[k, c],
        )

    def across(k):
        def copy(into):
            c = 1 - core if into else core
            return pltpu.make_async_remote_copy(
                src_ref=cbuf.at[k, :, c],
                dst_ref=cbuf.at[k, :, c],
                send_sem=psend.at[k],
                recv_sem=precv.at[k],
                device_id=partner,
                device_id_type=pl.DeviceIdType.MESH,
            )

        return functools.partial(copy, False), functools.partial(copy, True)

    def first(h):
        two = ng // 2

        def pick(buf, i, j):
            return lambda p: buf.at[pl.ds(two * h, two), *((p if v is None else v) for v in (i, j))]

        def one(buf, i, j):
            return lambda p, k: buf.at[pl.ds(two * h + two // 2 * k, two // 2), *((p if v is None else v) for v in (i, j))]

        q = ring_stage(
            pick(qbuf, y, None), one(qbuf, y, None), x, nx, at_x,
            lambda c: fsend.at[h, 0, c], lambda c: frecv.at[h, 0, c],
        )
        p = ring_stage(
            pick(pbuf, None, x), one(pbuf, None, x), y, ny, at_y,
            lambda c: fsend.at[h, 1, c], lambda c: frecv.at[h, 1, c],
        )
        return q, p

    def second(i):
        q = ring_stage(
            lambda p: qbuf.at[i, p], lambda p, h: qbuf.at[i, p, pl.ds(nx // 2 * h, nx // 2)], y, ny, at_y,
            lambda c: gsend.at[i, 0, c], lambda c: grecv.at[i, 0, c],
        )
        p = ring_stage(
            lambda p: pbuf.at[i, :, p], lambda p, h: pbuf.at[i, pl.ds(ny // 2 * h, ny // 2), p], x, nx, at_x,
            lambda c: gsend.at[i, 1, c], lambda c: grecv.at[i, 1, c],
        )
        return q, p

    def each(stages, act):
        for stage in stages:
            act(stage)

    for copy in own:
        copy.wait()
    pl.semaphore_wait(barrier, len(near))
    begin(panel(0))
    begin(panel(1))
    each(first(0), begin)
    each(first(1), begin)
    for_tiles(lambda i: load_v(i).start())
    for_tiles(lambda i: load_u(i).start())
    forward(panel(0))
    forward(panel(1))
    each(first(0), forward)
    each(first(1), forward)
    for k in range(2):
        arrived(panel(k))
        across(k)[0]().start()
    each(first(0), arrived)
    for_groups(0, lambda n: each(second(n), begin))
    each(first(1), arrived)

    r, c = iota((w, w), 0), iota((w, w), 1)
    order = u_ref.shape[1]

    def project(i):
        load_v(i).wait()
        a_ref[i] = jnp.where(r < trank[i], tdot(vbuf[i], s_ref[...]), 0.0).astype(bf16)

    for_tiles(project)
    for k in range(2):
        across(k)[1]().wait_recv()
    for_groups(0, lambda n: each(second(n), forward))
    for_groups(1, lambda n: each(second(n), begin))
    xs = cbuf[1].reshape(order, w)
    side_ref[0] = xs
    px_ref[...] = jnp.where(r < crank[0], -tdot(xs, s_ref[...]), 0.0).astype(bf16)

    def math(n, k):
        i = n * g + k
        core_ij = tdot(qbuf[n, :, :, k].reshape(order, w), cbuf[0].reshape(order, w))
        core_ij = jnp.where((r < rrank[i]) & (c < crank[0]), core_ij, 0.0).astype(bf16)
        left = ndot(pbuf[n, :, :, k].reshape(order, w), core_ij).astype(bf16)
        lbuf[i] = left
        load_u(i).wait()
        both = jnp.concatenate([ubuf[i], left], axis=1)
        mbuf[i] = tdot(both, both)
        store_left(i).start()

    for h in range(2):

        def collect(n):
            each(second(n), arrived)
            lax.fori_loop(0, g, lambda k, carry: (math(n, k), carry)[1], 0)

        if h == 1:
            for_groups(1, lambda n: each(second(n), forward))
        for_groups(h, collect)
        if h == 0:
            cmats = [jnp.concatenate([a_ref[t], px_ref[...]], axis=0) for t in range(done)]
            for t in range(done):
                t_ref[t], f_ref[t] = prepare(cmats[t], mbuf[t])
            eliminate(f_ref, 0, done, w)
            for t in range(done):
                z_ref[t], rv_ref[t] = finish(order, trank[t], crank[0], listed[t] == 1, cmats[t], f_ref[t], t_ref[t])

    m_ref[...] = mbuf[done:]
    for k in range(2):
        sent(panel(k))
        across(k)[0]().wait_send()
    for h in range(2):
        each(first(h), sent)
        for_groups(h, lambda n: each(second(n), sent))
    for_tiles(lambda i: store_left(i).wait())


def eliminate_block(parts, q0, base, nt, w):
    lane, sub, n = iota((1, 1, w), 2), iota((1, 8, 1), 1), len(parts)
    cols = {q: [jnp.broadcast_to(parts[q][:, :, base + c : base + c + 1], (nt, 8, w)) for c in range(8)] for q in range(q0, n)}
    head = cols[q0]
    for i in range(0, 8, 2):
        j = i + 1
        on_i, on_j = lane == base + i, lane == base + j
        a, b, d = head[i][:, i:j], head[j][:, i:j], head[j][:, j : j + 1]
        inv_i = 1.0 / a
        inv_j = a * (1.0 / (a * d - b * b))
        ratio = b * inv_i
        row_i = jnp.where(on_i, 1.0, parts[q0][:, i:j]) * inv_i
        new_j = jnp.where(on_i, 0.0, parts[q0][:, j : j + 1]) - b * row_i
        row_j = jnp.where(on_j, 1.0, new_j) * inv_j
        row_i = jnp.where(on_j, 0.0, row_i)
        to_i = {c: head[c][:, i:j] * inv_i for c in range(j + 1, 8)}
        to_j = {c: (head[c][:, j : j + 1] - b * to_i[c]) * inv_j for c in range(j + 1, 8)}
        for q in range(q0, n):
            mul_i, mul_j = cols[q][i], cols[q][j] - cols[q][i] * ratio
            clear = on_i | on_j
            if q == q0:
                clear = clear & (sub > j)
                mul_i, mul_j = jnp.where(sub > j, mul_i, 0.0), jnp.where(sub > j, mul_j, 0.0)
            rows = jnp.where(clear, 0.0, parts[q]) - mul_i * row_i - mul_j * row_j
            parts[q] = jnp.where(sub == j, new_j, rows) if q == q0 else rows
            for c in range(j + 1, 8):
                cols[q][c] = cols[q][c] - mul_i * to_i[c] - mul_j * to_j[c]


def eliminate(f_ref, t0, nt, w, between=lambda: None):
    lane2, row2 = iota((NB, w), 1), iota((NB, w), 0)
    for r0 in range(0, w, NB):
        spots = [(pl.ds(t0, nt), pl.ds(r0 + 8 * q, 8)) for q in range(NB // 8)]
        parts = [f_ref[spot] for spot in spots]
        for q0 in range(NB // 8):
            eliminate_block(parts, q0, r0 + 8 * q0, nt, w)
            between()
        for spot, part in zip(spots, parts):
            f_ref[spot] = part
        if r0 + NB == w:
            break
        inside = (lane2 >= r0) & (lane2 < r0 + NB)
        for t in range(t0, t0 + nt):
            panel = f_ref[t, r0 : r0 + NB, :]
            diag = jnp.sum(jnp.where(lane2 == row2 + r0, panel, 0.0), axis=1, keepdims=True)
            unit = jnp.where(lane2 - r0 < row2, panel, jnp.where(lane2 - r0 == row2, 1.0, 0.0))
            upd = lax.dot_general(
                panel * (1.0 / diag), jnp.where(inside, unit, panel), (((0,), (0,)), ((), ())),
                preferred_element_type=f32, precision=lax.Precision.HIGHEST,
            )[r0 + NB :, :]
            old = f_ref[t, r0 + NB :, :]
            lane = iota(old.shape, 1)
            f_ref[t, r0 + NB :, :] = jnp.where((lane >= r0) & (lane < r0 + NB), 0.0, old) - upd


def bt(a, b):
    return lax.dot_general(a, b, (((1,), (1,)), ((), ())), preferred_element_type=f32)


def prepare(cmat, m):
    w = cmat.shape[-1]
    r, c = iota((w, w), 0), iota((w, w), 1)
    mhi, mlo = split(m)
    tmat = ndot(mhi, cmat) + ndot(mlo, cmat)
    thi, tlo = split(tmat)
    gram = tdot(cmat, thi) + tdot(cmat, tlo)
    level = jnp.sum(jnp.where(r == c, gram, 0.0), axis=1, keepdims=True)
    level = jnp.sum(level, axis=0, keepdims=True) / w
    return tmat, gram + jnp.where(r == c, 0.01 * level + 1e-6, 0.0)


def finish(order, rank, crank, keep, cmat, fac, tmat):
    w = cmat.shape[-1]
    r, c = iota((w, w), 0), iota((w, w), 1)
    diag = jnp.sum(jnp.where(r == c, fac, 0.0), axis=1, keepdims=True)
    linv = (float(order) ** 0.5 * lax.rsqrt(diag)) * jnp.where(c < r, fac, jnp.where(c == r, 1.0, 0.0))
    lhi, llo = split(linv)
    thi, tlo = split(tmat)
    z = bt(cmat, lhi) + bt(cmat, llo)
    coef = (bt(thi, lhi) + bt(tlo, lhi) + bt(thi, llo)) * (1.0 / order)
    coef1 = jnp.where(r < rank, coef[:w], 0.0)
    coef2 = jnp.where(r < crank, coef[w:], 0.0)
    eye = jnp.where((r == c) & (r < rank), 1.0, 0.0)
    shift = jnp.where((c == r + rank) & (r < crank), 1.0, 0.0)
    zhi, zlo = split(jnp.concatenate([jnp.where(keep, z[:w], eye), jnp.where(keep, z[w:], shift)], axis=0))
    rv = jnp.concatenate([jnp.where(keep, coef1, eye), -jnp.where(keep, coef2, shift)], axis=0)
    return jnp.concatenate([zhi, zlo], axis=1), rv.astype(bf16)


def back_kernel(
    trank, crank, listed, m_ref, a_ref, px_ref, x_ref, z_ref, rv_ref, u_ref, left_ref, v_ref, ou_ref, ov_ref,
    ubuf, lbuf, vbuf, obuf, pbuf, zbuf, rbuf, f_ref, t_ref, isem, osem
):
    nt, order, w = u_ref.shape
    done = z_ref.shape[0]
    rest = nt - done
    loads = [
        [pltpu.make_async_copy(src.at[t], dst.at[t], isem.at[k, t]) for k, (src, dst) in enumerate(pairs)]
        for t, pairs in ((t, ((u_ref, ubuf), (left_ref, lbuf), (v_ref, vbuf))) for t in range(nt))
    ]
    for tile in loads:
        for copy in tile:
            copy.start()
    outs = [
        [pltpu.make_async_copy(src.at[t], dst.at[t], osem.at[k, t]) for k, (src, dst) in enumerate(((obuf, ou_ref), (pbuf, ov_ref)))]
        for t in range(nt)
    ]

    def cmat(t):
        return jnp.concatenate([a_ref[t], px_ref[...]], axis=0)

    for k in range(rest):
        t_ref[k], f_ref[k] = prepare(cmat(done + k), m_ref[k])

    def back(t, z, rv, h, pieces):
        rows = pl.ds(h * (order // pieces), order // pieces)
        both = ndot(jnp.concatenate([ubuf[t, rows], lbuf[t, rows]], axis=1), z)
        obuf[t, rows] = (both[:, :w] + both[:, w:]).astype(bf16)
        pbuf[t, rows] = ndot(jnp.concatenate([vbuf[t, rows], x_ref[0, rows]], axis=1), rv).astype(bf16)

    for t in range(done):
        for copy in loads[t]:
            copy.wait()
    todo = [(t, h) for t in range(done) for h in range(PIECES)]
    calls = w // 8
    share = -(-len(todo) // calls)

    def between():
        for _ in range(share):
            if todo:
                t, h = todo.pop(0)
                back(t, z_ref[t], rv_ref[t], h, PIECES)
                if h == PIECES - 1:
                    for copy in outs[t]:
                        copy.start()

    eliminate(f_ref, 0, rest, w, between)
    for k in range(rest):
        t = done + k
        zbuf[k], rbuf[k] = finish(order, trank[t], crank[0], listed[t] == 1, cmat(t), f_ref[k], t_ref[k])
    for t in range(done, nt):
        for copy in loads[t]:
            copy.wait()
        back(t, zbuf[t - done], rbuf[t - done], 0, 1)
        for copy in outs[t]:
            copy.start()
    for tile in outs:
        for copy in tile:
            copy.wait()


def front(mesh_sizes, done, u, v, trank, listed, row_u, row_v, rrank, col_u, col_v, crank, sketch):
    nt, order, w = u.shape
    nz, nc, ny, nx = mesh_sizes
    g = 2
    ng = nt // g
    row_u, row_v = (a.reshape(ng, g, *a.shape[1:]) for a in (row_u, row_v))
    smem = pl.BlockSpec(memory_space=pltpu.SMEM)
    vmem = pl.BlockSpec(memory_space=pltpu.VMEM)
    hbm = pl.BlockSpec(memory_space=pl.ANY)
    dma = pltpu.SemaphoreType.DMA
    return pl.pallas_call(
        functools.partial(gather_kernel, mesh_sizes),
        out_shape=(
            jax.ShapeDtypeStruct((nt - done, 2 * w, 2 * w), f32),
            jax.ShapeDtypeStruct((nt, w, w), bf16),
            jax.ShapeDtypeStruct((w, w), bf16),
            jax.ShapeDtypeStruct((nt, order, w), bf16),
            jax.ShapeDtypeStruct((1, order, w), bf16),
            jax.ShapeDtypeStruct((done, 2 * w, 2 * w), bf16),
            jax.ShapeDtypeStruct((done, 2 * w, w), bf16),
        ),
        in_specs=[smem, smem, smem, smem, hbm, hbm, hbm, hbm, hbm, hbm, vmem],
        out_specs=(vmem, vmem, vmem, hbm, vmem, vmem, vmem),
        scratch_shapes=[
            pltpu.VMEM((ng, ny, nx, g, w, w), bf16),
            pltpu.VMEM((ng, ny, nx, g, w, w), bf16),
            pltpu.VMEM((2, nz, nc, order // (nz * nc), w), bf16),
            pltpu.VMEM((nt, order, w), bf16),
            pltpu.VMEM((nt, order, w), bf16),
            pltpu.VMEM((nt, order, w), bf16),
            pltpu.VMEM((nt, 2 * w, 2 * w), f32),
            pltpu.VMEM((done, w, w), f32),
            pltpu.VMEM((done, 2 * w, w), f32),
            dma((4,)),
            dma((nt,)),
            dma((nt,)),
            dma((nt,)),
            dma((2, 2, 4)),
            dma((2, 2, 4)),
            dma((ng, 2, 4)),
            dma((ng, 2, 4)),
            dma((2, 4)),
            dma((2, 4)),
            dma((2,)),
            dma((2,)),
        ],
        compiler_params=pltpu.CompilerParams(collective_id=0, has_side_effects=True, vmem_limit_bytes=62 * 1024 * 1024),
    )(trank, rrank, crank, listed, row_u, row_v, col_u, col_v, u, v, sketch)


def back(u, v, trank, listed, crank, m, a, px, left, side_u, z, rv):
    nt, order, w = u.shape
    rest = nt - z.shape[0]
    smem = pl.BlockSpec(memory_space=pltpu.SMEM)
    vmem = pl.BlockSpec(memory_space=pltpu.VMEM)
    hbm = pl.BlockSpec(memory_space=pl.ANY)
    return pl.pallas_call(
        back_kernel,
        out_shape=(jax.ShapeDtypeStruct(u.shape, bf16), jax.ShapeDtypeStruct(u.shape, bf16)),
        in_specs=[smem, smem, smem, vmem, vmem, vmem, vmem, vmem, vmem, hbm, hbm, hbm],
        out_specs=(hbm, hbm),
        scratch_shapes=[pltpu.VMEM((nt, order, w), bf16)] * 5
        + [
            pltpu.VMEM((rest, 2 * w, 2 * w), bf16),
            pltpu.VMEM((rest, 2 * w, w), bf16),
            pltpu.VMEM((rest, w, w), f32),
            pltpu.VMEM((rest, 2 * w, w), f32),
            pltpu.SemaphoreType.DMA((3, nt)),
            pltpu.SemaphoreType.DMA((2, nt)),
        ],
        compiler_params=pltpu.CompilerParams(vmem_limit_bytes=62 * 1024 * 1024),
    )(trank, crank, listed, m, a, px, side_u, z, rv, u, left, v)


def on_device(
    sizes, tile_u, tile_v, tile_rank, listed, row_u, row_v, row_rank, col_u, col_v, col_rank, sketch
):
    u, v, trank, flags = tile_u[:, 0], tile_v[:, 0], tile_rank[:, 0], listed[:, 0]
    done = u.shape[0] // 2
    m, a, px, left, side_u, z, rv = front(
        sizes, done, u, v, trank, flags, row_u, row_v, row_rank, col_u, col_v, col_rank, sketch
    )
    out_u, out_v = back(u, v, trank, flags, col_rank, m, a, px, left, side_u, z, rv)
    return (out_u[:, None], out_v[:, None])


def solution(mesh):
    return jax.shard_map(
        functools.partial(on_device, (mesh.shape["row"] // 2, 2, 4, mesh.shape["col"] // 4)),
        mesh=mesh,
        in_specs=(
            P("row", "col", None, None),
            P("row", "col", None, None),
            P("row", "col"),
            P("row", "col"),
            P("row", "col", None),
            P("row", "col", None),
            P("row"),
            P("col", "row", None),
            P("col", "row", None),
            P("col"),
            P(),
        ),
        out_specs=(P("row", "col", None, None), P("row", "col", None, None)),
        check_vma=False,
    )
```

```python
import functools

import jax
import jax.numpy as jnp
from jax import lax
from jax.experimental import pallas as pl
from jax.experimental.pallas import tpu as pltpu
from jax.sharding import PartitionSpec as P

f32 = jnp.float32
bf16 = jnp.bfloat16
NB = 32


def tdot(a, b):
    return lax.dot_general(a, b, (((0,), (0,)), ((), ())), preferred_element_type=f32)


def ndot(a, b):
    return lax.dot_general(a, b, (((1,), (0,)), ((), ())), preferred_element_type=f32)


def split(x):
    hi = x.astype(bf16)
    return hi, (x - hi.astype(f32)).astype(bf16)


def iota(shape, dim):
    return lax.broadcasted_iota(jnp.int32, shape, dim)


def ring_stage(blk, half, pos, n, device, sends, recvs):
    right, left = lax.rem(pos + 1, n), lax.rem(pos + n - 1, n)

    far = lax.rem(pos + 2, n)

    def copy(into, k):
        if k < 2:
            ref = blk((left, right)[k] if into else pos)
        else:
            ref = half(far if into else (left, right)[k - 2], k - 2)
        return pltpu.make_async_remote_copy(
            src_ref=ref,
            dst_ref=ref,
            send_sem=sends(k),
            recv_sem=recvs(k),
            device_id=device((right, left)[k % 2]),
            device_id_type=pl.DeviceIdType.MESH,
        )

    return functools.partial(copy, False), functools.partial(copy, True)


def begin(stage):
    stage[0](0).start()
    stage[0](1).start()


def forward(stage):
    stage[1](0).wait_recv()
    stage[0](2).start()
    stage[1](1).wait_recv()
    stage[0](3).start()


def arrived(stage):
    stage[1](2).wait_recv()
    stage[1](3).wait_recv()


def sent(stage):
    for k in range(4):
        stage[0](k).wait_send()


def gather_kernel(
    sizes, trank, rrank, crank, listed, rowu_ref, rowv_ref, colu_ref, colv_ref, u_ref, v_ref, s_ref, m_ref, a_ref, px_ref, left_ref, side_ref, preu_ref, prev_ref,
    qbuf, pbuf, cbuf, ubuf, vbuf, lbuf, mbuf, obu, obv, z_ref, rv_ref, f_ref, t_ref, local, osem, usem, vsem, lsem, fsend, frecv, gsend, grecv, csend, crecv, psend, precv
):
    nz, nc, ny, nx = sizes
    ng, g, w = qbuf.shape[0], qbuf.shape[3], u_ref.shape[-1]
    nt = ng * g
    done = obu.shape[0]
    row, col = lax.axis_index("row"), lax.axis_index("col")
    z, core = row // nc, lax.rem(row, nc)
    y, x = col // nx, lax.rem(col, nx)

    def at_x(px):
        return (row, y * nx + px)

    def at_y(py):
        return (row, py * nx + x)

    def at_z(pz):
        return (pz * nc + core, col)

    partner = (z * nc + (1 - core), col)
    near = [at_x(lax.rem(x + 1, nx)), at_x(lax.rem(x + nx - 1, nx)), at_y(lax.rem(y + 1, ny)), at_y(lax.rem(y + ny - 1, ny))]
    near += [at_z(lax.rem(z + 1, nz)), at_z(lax.rem(z + nz - 1, nz)), partner]
    barrier = pltpu.get_barrier_semaphore()
    for device in near:
        pl.semaphore_signal(barrier, inc=1, device_id=device, device_id_type=pl.DeviceIdType.MESH)

    own = [
        pltpu.make_async_copy(colv_ref.at[0], cbuf.at[0, z, core], local.at[0]),
        pltpu.make_async_copy(colu_ref.at[0], cbuf.at[1, z, core], local.at[1]),
        pltpu.make_async_copy(rowv_ref, qbuf.at[:, y, x], local.at[2]),
        pltpu.make_async_copy(rowu_ref, pbuf.at[:, y, x], local.at[3]),
    ]
    for copy in own:
        copy.start()

    def load_u(i):
        return pltpu.make_async_copy(u_ref.at[i], ubuf.at[i], usem.at[i])

    def load_v(i):
        return pltpu.make_async_copy(v_ref.at[i], vbuf.at[i], vsem.at[i])

    def store_left(i):
        return pltpu.make_async_copy(lbuf.at[i], left_ref.at[i - done], lsem.at[i])

    def store_out(k, t):
        return pltpu.make_async_copy((obu, obv)[k].at[t], (preu_ref, prev_ref)[k].at[t], osem.at[k, t])

    def for_tiles(body):
        lax.fori_loop(0, nt, lambda i, c: (body(i), c)[1], 0)

    def for_groups(h, body):
        lax.fori_loop(ng // 2 * h, ng // 2 * (h + 1), lambda i, c: (body(i), c)[1], 0)

    hc = cbuf.shape[3] // 2

    def panel(k):
        return ring_stage(
            lambda p: cbuf.at[k, p, core], lambda p, h: cbuf.at[k, p, core, pl.ds(hc * h, hc)], z, nz, at_z,
            lambda c: csend.at[k, c], lambda c: crecv.at[k, c],
        )

    def across(k):
        def copy(into):
            c = 1 - core if into else core
            return pltpu.make_async_remote_copy(
                src_ref=cbuf.at[k, :, c],
                dst_ref=cbuf.at[k, :, c],
                send_sem=psend.at[k],
                recv_sem=precv.at[k],
                device_id=partner,
                device_id_type=pl.DeviceIdType.MESH,
            )

        return functools.partial(copy, False), functools.partial(copy, True)

    def first(h):
        two = ng // 2

        def pick(buf, i, j):
            return lambda p: buf.at[pl.ds(two * h, two), *((p if v is None else v) for v in (i, j))]

        def one(buf, i, j):
            return lambda p, k: buf.at[pl.ds(two * h + two // 2 * k, two // 2), *((p if v is None else v) for v in (i, j))]

        q = ring_stage(
            pick(qbuf, y, None), one(qbuf, y, None), x, nx, at_x,
            lambda c: fsend.at[h, 0, c], lambda c: frecv.at[h, 0, c],
        )
        p = ring_stage(
            pick(pbuf, None, x), one(pbuf, None, x), y, ny, at_y,
            lambda c: fsend.at[h, 1, c], lambda c: frecv.at[h, 1, c],
        )
        return q, p

    def second(i):
        q = ring_stage(
            lambda p: qbuf.at[i, p], lambda p, h: qbuf.at[i, p, pl.ds(nx // 2 * h, nx // 2)], y, ny, at_y,
            lambda c: gsend.at[i, 0, c], lambda c: grecv.at[i, 0, c],
        )
        p = ring_stage(
            lambda p: pbuf.at[i, :, p], lambda p, h: pbuf.at[i, pl.ds(ny // 2 * h, ny // 2), p], x, nx, at_x,
            lambda c: gsend.at[i, 1, c], lambda c: grecv.at[i, 1, c],
        )
        return q, p

    def each(stages, act):
        for stage in stages:
            act(stage)

    for copy in own:
        copy.wait()
    pl.semaphore_wait(barrier, len(near))
    begin(panel(0))
    begin(panel(1))
    each(first(0), begin)
    each(first(1), begin)
    for_tiles(lambda i: load_v(i).start())
    for_tiles(lambda i: load_u(i).start())
    forward(panel(0))
    forward(panel(1))
    each(first(0), forward)
    each(first(1), forward)
    for k in range(2):
        arrived(panel(k))
        across(k)[0]().start()
    each(first(0), arrived)
    for_groups(0, lambda n: each(second(n), begin))
    each(first(1), arrived)

    r, c = iota((w, w), 0), iota((w, w), 1)
    order = u_ref.shape[1]

    def project(i):
        load_v(i).wait()
        a_ref[i] = jnp.where(r < trank[i], tdot(vbuf[i], s_ref[...]), 0.0).astype(bf16)

    for_tiles(project)
    for k in range(2):
        across(k)[1]().wait_recv()
    for_groups(0, lambda n: each(second(n), forward))
    for_groups(1, lambda n: each(second(n), begin))
    xs = cbuf[1].reshape(order, w)
    side_ref[0] = xs
    px_ref[...] = jnp.where(r < crank[0], -tdot(xs, s_ref[...]), 0.0).astype(bf16)

    def math(n, k):
        i = n * g + k
        core_ij = tdot(qbuf[n, :, :, k].reshape(order, w), cbuf[0].reshape(order, w))
        core_ij = jnp.where((r < rrank[i]) & (c < crank[0]), core_ij, 0.0).astype(bf16)
        left = ndot(pbuf[n, :, :, k].reshape(order, w), core_ij).astype(bf16)
        lbuf[i] = left
        load_u(i).wait()
        both = jnp.concatenate([ubuf[i], left], axis=1)
        mbuf[i] = tdot(both, both)

        @pl.when(i >= done)
        def _():
            store_left(i).start()

    def early(t):
        both = ndot(jnp.concatenate([ubuf[t], lbuf[t]], axis=1), z_ref[t])
        obu[t] = (both[:, :w] + both[:, w:]).astype(bf16)
        obv[t] = ndot(jnp.concatenate([vbuf[t], cbuf[1].reshape(order, w)], axis=1), rv_ref[t]).astype(bf16)
        store_out(0, t).start()
        store_out(1, t).start()

    for h in range(2):

        def collect(n):
            each(second(n), arrived)
            for k in range(g):
                math(n, k)

        if h == 1:
            for_groups(1, lambda n: each(second(n), forward))
            lax.fori_loop(0, done, lambda t, carry: (early(t), carry)[1], 0)
        for_groups(h, collect)
        if h == 0:
            cmats = [jnp.concatenate([a_ref[t], px_ref[...]], axis=0) for t in range(done)]
            for t in range(done):
                t_ref[t], f_ref[t] = prepare(cmats[t], mbuf[t])
            eliminate(f_ref, 0, done, w)
            for t in range(done):
                z_ref[t], rv_ref[t] = finish(order, trank[t], crank[0], listed[t] == 1, cmats[t], f_ref[t], t_ref[t])

    m_ref[...] = mbuf[done:]
    for k in range(2):
        sent(panel(k))
        across(k)[0]().wait_send()
    for h in range(2):
        each(first(h), sent)
        for_groups(h, lambda n: each(second(n), sent))
    lax.fori_loop(0, done, lambda t, carry: (store_out(0, t).wait(), store_out(1, t).wait(), carry)[2], 0)
    lax.fori_loop(done, nt, lambda t, carry: (store_left(t).wait(), carry)[1], 0)


def eliminate_block(parts, q0, base, nt, w):
    lane, sub, n = iota((1, 1, w), 2), iota((1, 8, 1), 1), len(parts)
    cols = {q: [jnp.broadcast_to(parts[q][:, :, base + c : base + c + 1], (nt, 8, w)) for c in range(8)] for q in range(q0, n)}
    head = cols[q0]
    for i in range(0, 8, 2):
        j = i + 1
        on_i, on_j = lane == base + i, lane == base + j
        a, b, d = head[i][:, i:j], head[j][:, i:j], head[j][:, j : j + 1]
        inv_i = 1.0 / a
        inv_j = a * (1.0 / (a * d - b * b))
        ratio = b * inv_i
        row_i = jnp.where(on_i, 1.0, parts[q0][:, i:j]) * inv_i
        new_j = jnp.where(on_i, 0.0, parts[q0][:, j : j + 1]) - b * row_i
        row_j = jnp.where(on_j, 1.0, new_j) * inv_j
        row_i = jnp.where(on_j, 0.0, row_i)
        to_i = {c: head[c][:, i:j] * inv_i for c in range(j + 1, 8)}
        to_j = {c: (head[c][:, j : j + 1] - b * to_i[c]) * inv_j for c in range(j + 1, 8)}
        for q in range(q0, n):
            mul_i, mul_j = cols[q][i], cols[q][j] - cols[q][i] * ratio
            clear = on_i | on_j
            if q == q0:
                clear = clear & (sub > j)
                mul_i, mul_j = jnp.where(sub > j, mul_i, 0.0), jnp.where(sub > j, mul_j, 0.0)
            rows = jnp.where(clear, 0.0, parts[q]) - mul_i * row_i - mul_j * row_j
            parts[q] = jnp.where(sub == j, new_j, rows) if q == q0 else rows
            for c in range(j + 1, 8):
                cols[q][c] = cols[q][c] - mul_i * to_i[c] - mul_j * to_j[c]


def eliminate(f_ref, t0, nt, w):
    lane2, row2 = iota((NB, w), 1), iota((NB, w), 0)
    for r0 in range(0, w, NB):
        spots = [(pl.ds(t0, nt), pl.ds(r0 + 8 * q, 8)) for q in range(NB // 8)]
        parts = [f_ref[spot] for spot in spots]
        for q0 in range(NB // 8):
            eliminate_block(parts, q0, r0 + 8 * q0, nt, w)
        for spot, part in zip(spots, parts):
            f_ref[spot] = part
        if r0 + NB == w:
            break
        inside = (lane2 >= r0) & (lane2 < r0 + NB)
        for t in range(t0, t0 + nt):
            panel = f_ref[t, r0 : r0 + NB, :]
            diag = jnp.sum(jnp.where(lane2 == row2 + r0, panel, 0.0), axis=1, keepdims=True)
            unit = jnp.where(lane2 - r0 < row2, panel, jnp.where(lane2 - r0 == row2, 1.0, 0.0))
            upd = lax.dot_general(
                panel * (1.0 / diag), jnp.where(inside, unit, panel), (((0,), (0,)), ((), ())),
                preferred_element_type=f32, precision=lax.Precision.HIGHEST,
            )[r0 + NB :, :]
            old = f_ref[t, r0 + NB :, :]
            lane = iota(old.shape, 1)
            f_ref[t, r0 + NB :, :] = jnp.where((lane >= r0) & (lane < r0 + NB), 0.0, old) - upd


def bt(a, b):
    return lax.dot_general(a, b, (((1,), (1,)), ((), ())), preferred_element_type=f32)


def prepare(cmat, m):
    w = cmat.shape[-1]
    r, c = iota((w, w), 0), iota((w, w), 1)
    mhi, mlo = split(m)
    tmat = ndot(mhi, cmat) + ndot(mlo, cmat)
    thi, tlo = split(tmat)
    gram = tdot(cmat, thi) + tdot(cmat, tlo)
    level = jnp.sum(jnp.where(r == c, gram, 0.0), axis=1, keepdims=True)
    level = jnp.sum(level, axis=0, keepdims=True) / w
    return tmat, gram + jnp.where(r == c, 0.01 * level + 1e-6, 0.0)


def finish(order, rank, crank, keep, cmat, fac, tmat):
    w = cmat.shape[-1]
    r, c = iota((w, w), 0), iota((w, w), 1)
    diag = jnp.sum(jnp.where(r == c, fac, 0.0), axis=1, keepdims=True)
    linv = (float(order) ** 0.5 * lax.rsqrt(diag)) * jnp.where(c < r, fac, jnp.where(c == r, 1.0, 0.0))
    lhi, llo = split(linv)
    thi, tlo = split(tmat)
    z = bt(cmat, lhi) + bt(cmat, llo)
    coef = (bt(thi, lhi) + bt(tlo, lhi) + bt(thi, llo)) * (1.0 / order)
    coef1 = jnp.where(r < rank, coef[:w], 0.0)
    coef2 = jnp.where(r < crank, coef[w:], 0.0)
    eye = jnp.where((r == c) & (r < rank), 1.0, 0.0)
    shift = jnp.where((c == r + rank) & (r < crank), 1.0, 0.0)
    zhi, zlo = split(jnp.concatenate([jnp.where(keep, z[:w], eye), jnp.where(keep, z[w:], shift)], axis=0))
    rv = jnp.concatenate([jnp.where(keep, coef1, eye), -jnp.where(keep, coef2, shift)], axis=0)
    return jnp.concatenate([zhi, zlo], axis=1), rv.astype(bf16)


def back_kernel(
    trank, crank, listed, m_ref, a_ref, px_ref, x_ref, u_ref, left_ref, v_ref, preu_ref, prev_ref, ou_ref, ov_ref,
    ubuf, lbuf, vbuf, obu, obv, f_ref, t_ref, isem, osem
):
    nt, order, w = u_ref.shape
    done = preu_ref.shape[0]
    rest = nt - done

    def copies(t):
        if t < done:
            return [
                pltpu.make_async_copy(preu_ref.at[t], obu.at[t], isem.at[0, t]),
                pltpu.make_async_copy(prev_ref.at[t], obv.at[t], isem.at[1, t]),
            ]
        k = t - done
        return [
            pltpu.make_async_copy(u_ref.at[t], ubuf.at[k], isem.at[0, t]),
            pltpu.make_async_copy(left_ref.at[k], lbuf.at[k], isem.at[1, t]),
            pltpu.make_async_copy(v_ref.at[t], vbuf.at[k], isem.at[2, t]),
        ]

    def store(t):
        return [
            pltpu.make_async_copy(obu.at[t], ou_ref.at[t], osem.at[0, t]),
            pltpu.make_async_copy(obv.at[t], ov_ref.at[t], osem.at[1, t]),
        ]

    loads = [copies(t) for t in range(nt)]
    outs = [store(t) for t in range(nt)]
    for t in range(nt):
        for copy in loads[t]:
            copy.start()

    def cmat(t):
        return jnp.concatenate([a_ref[t], px_ref[...]], axis=0)

    for k in range(rest):
        t_ref[k], f_ref[k] = prepare(cmat(done + k), m_ref[k])
    for t in range(done):
        for copy in loads[t]:
            copy.wait()
        for copy in outs[t]:
            copy.start()
    eliminate(f_ref, 0, rest, w)
    for t in range(done, nt):
        for copy in loads[t]:
            copy.wait()
    for k in range(rest):
        t = done + k
        z, rv = finish(order, trank[t], crank[0], listed[t] == 1, cmat(t), f_ref[k], t_ref[k])
        both = ndot(jnp.concatenate([ubuf[k], lbuf[k]], axis=1), z)
        obu[t] = (both[:, :w] + both[:, w:]).astype(bf16)
        obv[t] = ndot(jnp.concatenate([vbuf[k], x_ref[0]], axis=1), rv).astype(bf16)
        for copy in outs[t]:
            copy.start()
    for tile in outs:
        for copy in tile:
            copy.wait()


def front(mesh_sizes, done, u, v, trank, listed, row_u, row_v, rrank, col_u, col_v, crank, sketch):
    nt, order, w = u.shape
    nz, nc, ny, nx = mesh_sizes
    g = 2
    ng = nt // g
    row_u, row_v = (a.reshape(ng, g, *a.shape[1:]) for a in (row_u, row_v))
    smem = pl.BlockSpec(memory_space=pltpu.SMEM)
    vmem = pl.BlockSpec(memory_space=pltpu.VMEM)
    hbm = pl.BlockSpec(memory_space=pl.ANY)
    dma = pltpu.SemaphoreType.DMA
    return pl.pallas_call(
        functools.partial(gather_kernel, mesh_sizes),
        out_shape=(
            jax.ShapeDtypeStruct((nt - done, 2 * w, 2 * w), f32),
            jax.ShapeDtypeStruct((nt, w, w), bf16),
            jax.ShapeDtypeStruct((w, w), bf16),
            jax.ShapeDtypeStruct((nt - done, order, w), bf16),
            jax.ShapeDtypeStruct((1, order, w), bf16),
            jax.ShapeDtypeStruct((done, order, w), bf16),
            jax.ShapeDtypeStruct((done, order, w), bf16),
        ),
        in_specs=[smem, smem, smem, smem, hbm, hbm, hbm, hbm, hbm, hbm, vmem],
        out_specs=(vmem, vmem, vmem, hbm, vmem, hbm, hbm),
        scratch_shapes=[
            pltpu.VMEM((ng, ny, nx, g, w, w), bf16),
            pltpu.VMEM((ng, ny, nx, g, w, w), bf16),
            pltpu.VMEM((2, nz, nc, order // (nz * nc), w), bf16),
            pltpu.VMEM((nt, order, w), bf16),
            pltpu.VMEM((nt, order, w), bf16),
            pltpu.VMEM((nt, order, w), bf16),
            pltpu.VMEM((nt, 2 * w, 2 * w), f32),
            pltpu.VMEM((done, order, w), bf16),
            pltpu.VMEM((done, order, w), bf16),
            pltpu.VMEM((done, 2 * w, 2 * w), bf16),
            pltpu.VMEM((done, 2 * w, w), bf16),
            pltpu.VMEM((done, w, w), f32),
            pltpu.VMEM((done, 2 * w, w), f32),
            dma((4,)),
            dma((2, done)),
            dma((nt,)),
            dma((nt,)),
            dma((nt,)),
            dma((2, 2, 4)),
            dma((2, 2, 4)),
            dma((ng, 2, 4)),
            dma((ng, 2, 4)),
            dma((2, 4)),
            dma((2, 4)),
            dma((2,)),
            dma((2,)),
        ],
        compiler_params=pltpu.CompilerParams(collective_id=0, has_side_effects=True, vmem_limit_bytes=62 * 1024 * 1024),
    )(trank, rrank, crank, listed, row_u, row_v, col_u, col_v, u, v, sketch)


def back(u, v, trank, listed, crank, m, a, px, left, side_u, pre_u, pre_v):
    nt, order, w = u.shape
    rest = nt - pre_u.shape[0]
    smem = pl.BlockSpec(memory_space=pltpu.SMEM)
    vmem = pl.BlockSpec(memory_space=pltpu.VMEM)
    hbm = pl.BlockSpec(memory_space=pl.ANY)
    return pl.pallas_call(
        back_kernel,
        out_shape=(jax.ShapeDtypeStruct(u.shape, bf16), jax.ShapeDtypeStruct(u.shape, bf16)),
        in_specs=[smem, smem, smem, vmem, vmem, vmem, vmem, hbm, hbm, hbm, hbm, hbm],
        out_specs=(hbm, hbm),
        scratch_shapes=[pltpu.VMEM((rest, order, w), bf16)] * 3
        + [pltpu.VMEM((nt, order, w), bf16)] * 2
        + [
            pltpu.VMEM((rest, w, w), f32),
            pltpu.VMEM((rest, 2 * w, w), f32),
            pltpu.SemaphoreType.DMA((3, nt)),
            pltpu.SemaphoreType.DMA((2, nt)),
        ],
        compiler_params=pltpu.CompilerParams(vmem_limit_bytes=62 * 1024 * 1024),
    )(trank, crank, listed, m, a, px, side_u, u, left, v, pre_u, pre_v)


def on_device(
    sizes, tile_u, tile_v, tile_rank, listed, row_u, row_v, row_rank, col_u, col_v, col_rank, sketch
):
    u, v, trank, flags = tile_u[:, 0], tile_v[:, 0], tile_rank[:, 0], listed[:, 0]
    done = u.shape[0] // 2
    m, a, px, left, side_u, pre_u, pre_v = front(
        sizes, done, u, v, trank, flags, row_u, row_v, row_rank, col_u, col_v, col_rank, sketch
    )
    out_u, out_v = back(u, v, trank, flags, col_rank, m, a, px, left, side_u, pre_u, pre_v)
    return (out_u[:, None], out_v[:, None])


def solution(mesh):
    return jax.shard_map(
        functools.partial(on_device, (mesh.shape["row"] // 2, 2, 4, mesh.shape["col"] // 4)),
        mesh=mesh,
        in_specs=(
            P("row", "col", None, None),
            P("row", "col", None, None),
            P("row", "col"),
            P("row", "col"),
            P("row", "col", None),
            P("row", "col", None),
            P("row"),
            P("col", "row", None),
            P("col", "row", None),
            P("col"),
            P(),
        ),
        out_specs=(P("row", "col", None, None), P("row", "col", None, None)),
        check_vma=False,
    )
```

```python
import functools

import jax
import jax.numpy as jnp
from jax import lax
from jax.experimental import pallas as pl
from jax.experimental.pallas import tpu as pltpu
from jax.sharding import PartitionSpec as P

f32 = jnp.float32
bf16 = jnp.bfloat16
NB = 32


def tdot(a, b):
    return lax.dot_general(a, b, (((0,), (0,)), ((), ())), preferred_element_type=f32)


def ndot(a, b):
    return lax.dot_general(a, b, (((1,), (0,)), ((), ())), preferred_element_type=f32)


def split(x):
    hi = x.astype(bf16)
    return hi, (x - hi.astype(f32)).astype(bf16)


def iota(shape, dim):
    return lax.broadcasted_iota(jnp.int32, shape, dim)


def ring_stage(blk, half, pos, n, device, sends, recvs):
    right, left = lax.rem(pos + 1, n), lax.rem(pos + n - 1, n)

    far = lax.rem(pos + 2, n)

    def copy(into, k):
        if k < 2:
            ref = blk((left, right)[k] if into else pos)
        else:
            ref = half(far if into else (left, right)[k - 2], k - 2)
        return pltpu.make_async_remote_copy(
            src_ref=ref,
            dst_ref=ref,
            send_sem=sends(k),
            recv_sem=recvs(k),
            device_id=device((right, left)[k % 2]),
            device_id_type=pl.DeviceIdType.MESH,
        )

    return functools.partial(copy, False), functools.partial(copy, True)


def begin(stage):
    stage[0](0).start()
    stage[0](1).start()


def forward(stage):
    stage[1](0).wait_recv()
    stage[0](2).start()
    stage[1](1).wait_recv()
    stage[0](3).start()


def arrived(stage):
    stage[1](2).wait_recv()
    stage[1](3).wait_recv()


def sent(stage):
    for k in range(4):
        stage[0](k).wait_send()


def gather_kernel(
    sizes, trank, rrank, crank, listed, rowu_ref, rowv_ref, colu_ref, colv_ref, u_ref, v_ref, s_ref, m_ref, a_ref, px_ref, left_ref, side_ref, preu_ref, prev_ref,
    qbuf, pbuf, cbuf, ubuf, vbuf, lbuf, mbuf, obu, obv, z_ref, rv_ref, f_ref, t_ref, local, osem, usem, vsem, lsem, msem, fsend, frecv, gsend, grecv, csend, crecv, psend, precv
):
    nz, nc, ny, nx = sizes
    ng, g, w = qbuf.shape[0], qbuf.shape[3], u_ref.shape[-1]
    nt = ng * g
    done = obu.shape[0]
    row, col = lax.axis_index("row"), lax.axis_index("col")
    z, core = row // nc, lax.rem(row, nc)
    y, x = col // nx, lax.rem(col, nx)

    def at_x(px):
        return (row, y * nx + px)

    def at_y(py):
        return (row, py * nx + x)

    def at_z(pz):
        return (pz * nc + core, col)

    partner = (z * nc + (1 - core), col)
    near = [at_x(lax.rem(x + 1, nx)), at_x(lax.rem(x + nx - 1, nx)), at_y(lax.rem(y + 1, ny)), at_y(lax.rem(y + ny - 1, ny))]
    near += [at_z(lax.rem(z + 1, nz)), at_z(lax.rem(z + nz - 1, nz)), partner]
    barrier = pltpu.get_barrier_semaphore()
    for device in near:
        pl.semaphore_signal(barrier, inc=1, device_id=device, device_id_type=pl.DeviceIdType.MESH)

    own = [
        pltpu.make_async_copy(colv_ref.at[0], cbuf.at[0, z, core], local.at[0]),
        pltpu.make_async_copy(colu_ref.at[0], cbuf.at[1, z, core], local.at[1]),
        pltpu.make_async_copy(rowv_ref, qbuf.at[:, y, x], local.at[2]),
        pltpu.make_async_copy(rowu_ref, pbuf.at[:, y, x], local.at[3]),
    ]
    for copy in own:
        copy.start()

    def load_u(i):
        return pltpu.make_async_copy(u_ref.at[i], ubuf.at[i], usem.at[i])

    def load_v(i):
        return pltpu.make_async_copy(v_ref.at[i], vbuf.at[i], vsem.at[i])

    def store_left(i):
        return pltpu.make_async_copy(lbuf.at[i], left_ref.at[i - done], lsem.at[i])

    def store_m(i):
        return pltpu.make_async_copy(mbuf.at[i], m_ref.at[i - done], msem.at[i])

    def store_out(k, t):
        return pltpu.make_async_copy((obu, obv)[k].at[t], (preu_ref, prev_ref)[k].at[t], osem.at[k, t])

    def for_tiles(body):
        lax.fori_loop(0, nt, lambda i, c: (body(i), c)[1], 0)

    def for_groups(h, body):
        lax.fori_loop(ng // 2 * h, ng // 2 * (h + 1), lambda i, c: (body(i), c)[1], 0)

    hc = cbuf.shape[3] // 2

    def panel(k):
        return ring_stage(
            lambda p: cbuf.at[k, p, core], lambda p, h: cbuf.at[k, p, core, pl.ds(hc * h, hc)], z, nz, at_z,
            lambda c: csend.at[k, c], lambda c: crecv.at[k, c],
        )

    def across(k):
        def copy(into):
            c = 1 - core if into else core
            return pltpu.make_async_remote_copy(
                src_ref=cbuf.at[k, :, c],
                dst_ref=cbuf.at[k, :, c],
                send_sem=psend.at[k],
                recv_sem=precv.at[k],
                device_id=partner,
                device_id_type=pl.DeviceIdType.MESH,
            )

        return functools.partial(copy, False), functools.partial(copy, True)

    def first(h):
        two = ng // 2

        def pick(buf, i, j):
            return lambda p: buf.at[pl.ds(two * h, two), *((p if v is None else v) for v in (i, j))]

        def one(buf, i, j):
            return lambda p, k: buf.at[pl.ds(two * h + two // 2 * k, two // 2), *((p if v is None else v) for v in (i, j))]

        q = ring_stage(
            pick(qbuf, y, None), one(qbuf, y, None), x, nx, at_x,
            lambda c: fsend.at[h, 0, c], lambda c: frecv.at[h, 0, c],
        )
        p = ring_stage(
            pick(pbuf, None, x), one(pbuf, None, x), y, ny, at_y,
            lambda c: fsend.at[h, 1, c], lambda c: frecv.at[h, 1, c],
        )
        return q, p

    def second(i):
        q = ring_stage(
            lambda p: qbuf.at[i, p], lambda p, h: qbuf.at[i, p, pl.ds(nx // 2 * h, nx // 2)], y, ny, at_y,
            lambda c: gsend.at[i, 0, c], lambda c: grecv.at[i, 0, c],
        )
        p = ring_stage(
            lambda p: pbuf.at[i, :, p], lambda p, h: pbuf.at[i, pl.ds(ny // 2 * h, ny // 2), p], x, nx, at_x,
            lambda c: gsend.at[i, 1, c], lambda c: grecv.at[i, 1, c],
        )
        return q, p

    def each(stages, act):
        for stage in stages:
            act(stage)

    for copy in own:
        copy.wait()
    pl.semaphore_wait(barrier, len(near))
    begin(panel(0))
    begin(panel(1))
    each(first(0), begin)
    each(first(1), begin)
    for_tiles(lambda i: load_v(i).start())
    for_tiles(lambda i: load_u(i).start())
    forward(panel(0))
    forward(panel(1))
    each(first(0), forward)
    each(first(1), forward)
    for k in range(2):
        arrived(panel(k))
        across(k)[0]().start()
    each(first(0), arrived)
    for_groups(0, lambda n: each(second(n), begin))
    each(first(1), arrived)

    r, c = iota((w, w), 0), iota((w, w), 1)
    order = u_ref.shape[1]

    def project(i):
        load_v(i).wait()
        a_ref[i] = jnp.where(r < trank[i], tdot(vbuf[i], s_ref[...]), 0.0).astype(bf16)

    for_tiles(project)
    for k in range(2):
        across(k)[1]().wait_recv()
    for_groups(0, lambda n: each(second(n), forward))
    for_groups(1, lambda n: each(second(n), begin))
    xs = cbuf[1].reshape(order, w)
    store_side = pltpu.make_async_copy(cbuf.at[1], side_ref, local.at[0])
    store_side.start()
    px_ref[...] = jnp.where(r < crank[0], -tdot(xs, s_ref[...]), 0.0).astype(bf16)

    def math(n, k):
        i = n * g + k
        core_ij = tdot(qbuf[n, :, :, k].reshape(order, w), cbuf[0].reshape(order, w))
        core_ij = jnp.where((r < rrank[i]) & (c < crank[0]), core_ij, 0.0).astype(bf16)
        left = ndot(pbuf[n, :, :, k].reshape(order, w), core_ij).astype(bf16)
        lbuf[i] = left
        load_u(i).wait()
        both = jnp.concatenate([ubuf[i], left], axis=1)
        mbuf[i] = tdot(both, both)

        @pl.when(i >= done)
        def _():
            store_left(i).start()
            store_m(i).start()

    def early(t):
        both = ndot(jnp.concatenate([ubuf[t], lbuf[t]], axis=1), z_ref[t])
        obu[t] = (both[:, :w] + both[:, w:]).astype(bf16)
        obv[t] = ndot(jnp.concatenate([vbuf[t], cbuf[1].reshape(order, w)], axis=1), rv_ref[t]).astype(bf16)
        store_out(0, t).start()
        store_out(1, t).start()

    for h in range(2):

        def collect(n):
            each(second(n), arrived)
            for k in range(g):
                math(n, k)

        if h == 1:
            for_groups(1, lambda n: each(second(n), forward))
            lax.fori_loop(0, done, lambda t, carry: (early(t), carry)[1], 0)
        for_groups(h, collect)
        if h == 0:
            cmats = [jnp.concatenate([a_ref[t], px_ref[...]], axis=0) for t in range(done)]
            for t in range(done):
                t_ref[t], f_ref[t] = prepare(cmats[t], mbuf[t])
            eliminate(f_ref, 0, done, w)
            for t in range(done):
                z_ref[t], rv_ref[t] = finish(order, trank[t], crank[0], listed[t] == 1, cmats[t], f_ref[t], t_ref[t])

    store_side.wait()
    for k in range(2):
        sent(panel(k))
        across(k)[0]().wait_send()
    for h in range(2):
        each(first(h), sent)
        for_groups(h, lambda n: each(second(n), sent))
    lax.fori_loop(0, done, lambda t, carry: (store_out(0, t).wait(), store_out(1, t).wait(), carry)[2], 0)
    lax.fori_loop(done, nt, lambda t, carry: (store_left(t).wait(), store_m(t).wait(), carry)[2], 0)


def eliminate_block(parts, q0, base, nt, w):
    lane, sub, n = iota((1, 1, w), 2), iota((1, 8, 1), 1), len(parts)
    cols = {q: [jnp.broadcast_to(parts[q][:, :, base + c : base + c + 1], (nt, 8, w)) for c in range(8)] for q in range(q0, n)}
    head = cols[q0]
    for i in range(0, 8, 2):
        j = i + 1
        on_i, on_j = lane == base + i, lane == base + j
        a, b, d = head[i][:, i:j], head[j][:, i:j], head[j][:, j : j + 1]
        inv_i = 1.0 / a
        inv_j = a * (1.0 / (a * d - b * b))
        ratio = b * inv_i
        row_i = jnp.where(on_i, 1.0, parts[q0][:, i:j]) * inv_i
        new_j = jnp.where(on_i, 0.0, parts[q0][:, j : j + 1]) - b * row_i
        row_j = jnp.where(on_j, 1.0, new_j) * inv_j
        row_i = jnp.where(on_j, 0.0, row_i)
        to_i = {c: head[c][:, i:j] * inv_i for c in range(j + 1, 8)}
        to_j = {c: (head[c][:, j : j + 1] - b * to_i[c]) * inv_j for c in range(j + 1, 8)}
        for q in range(q0, n):
            mul_i, mul_j = cols[q][i], cols[q][j] - cols[q][i] * ratio
            clear = on_i | on_j
            if q == q0:
                clear = clear & (sub > j)
                mul_i, mul_j = jnp.where(sub > j, mul_i, 0.0), jnp.where(sub > j, mul_j, 0.0)
            rows = jnp.where(clear, 0.0, parts[q]) - mul_i * row_i - mul_j * row_j
            parts[q] = jnp.where(sub == j, new_j, rows) if q == q0 else rows
            for c in range(j + 1, 8):
                cols[q][c] = cols[q][c] - mul_i * to_i[c] - mul_j * to_j[c]


def eliminate(f_ref, t0, nt, w):
    lane2, row2 = iota((NB, w), 1), iota((NB, w), 0)
    for r0 in range(0, w, NB):
        spots = [(pl.ds(t0, nt), pl.ds(r0 + 8 * q, 8)) for q in range(NB // 8)]
        parts = [f_ref[spot] for spot in spots]
        for q0 in range(NB // 8):
            eliminate_block(parts, q0, r0 + 8 * q0, nt, w)
        for spot, part in zip(spots, parts):
            f_ref[spot] = part
        if r0 + NB == w:
            break
        inside = (lane2 >= r0) & (lane2 < r0 + NB)
        for t in range(t0, t0 + nt):
            panel = f_ref[t, r0 : r0 + NB, :]
            diag = jnp.sum(jnp.where(lane2 == row2 + r0, panel, 0.0), axis=1, keepdims=True)
            unit = jnp.where(lane2 - r0 < row2, panel, jnp.where(lane2 - r0 == row2, 1.0, 0.0))
            upd = lax.dot_general(
                panel * (1.0 / diag), jnp.where(inside, unit, panel), (((0,), (0,)), ((), ())),
                preferred_element_type=f32, precision=lax.Precision.HIGHEST,
            )[r0 + NB :, :]
            old = f_ref[t, r0 + NB :, :]
            lane = iota(old.shape, 1)
            f_ref[t, r0 + NB :, :] = jnp.where((lane >= r0) & (lane < r0 + NB), 0.0, old) - upd


def bt(a, b):
    return lax.dot_general(a, b, (((1,), (1,)), ((), ())), preferred_element_type=f32)


def prepare(cmat, m):
    w = cmat.shape[-1]
    r, c = iota((w, w), 0), iota((w, w), 1)
    mhi, mlo = split(m)
    tmat = ndot(mhi, cmat) + ndot(mlo, cmat)
    thi, tlo = split(tmat)
    gram = tdot(cmat, thi) + tdot(cmat, tlo)
    level = jnp.sum(jnp.where(r == c, gram, 0.0), axis=1, keepdims=True)
    level = jnp.sum(level, axis=0, keepdims=True) / w
    return tmat, gram + jnp.where(r == c, 0.01 * level + 1e-6, 0.0)


def finish(order, rank, crank, keep, cmat, fac, tmat):
    w = cmat.shape[-1]
    r, c = iota((w, w), 0), iota((w, w), 1)
    diag = jnp.sum(jnp.where(r == c, fac, 0.0), axis=1, keepdims=True)
    linv = (float(order) ** 0.5 * lax.rsqrt(diag)) * jnp.where(c < r, fac, jnp.where(c == r, 1.0, 0.0))
    lhi, llo = split(linv)
    thi, tlo = split(tmat)
    z = bt(cmat, lhi) + bt(cmat, llo)
    coef = (bt(thi, lhi) + bt(tlo, lhi) + bt(thi, llo)) * (1.0 / order)
    coef1 = jnp.where(r < rank, coef[:w], 0.0)
    coef2 = jnp.where(r < crank, coef[w:], 0.0)
    eye = jnp.where((r == c) & (r < rank), 1.0, 0.0)
    shift = jnp.where((c == r + rank) & (r < crank), 1.0, 0.0)
    zhi, zlo = split(jnp.concatenate([jnp.where(keep, z[:w], eye), jnp.where(keep, z[w:], shift)], axis=0))
    rv = jnp.concatenate([jnp.where(keep, coef1, eye), -jnp.where(keep, coef2, shift)], axis=0)
    return jnp.concatenate([zhi, zlo], axis=1), rv.astype(bf16)


def back_kernel(
    trank, crank, listed, m_ref, a_ref, px_ref, x_ref, u_ref, left_ref, v_ref, preu_ref, prev_ref, ou_ref, ov_ref,
    ubuf, lbuf, vbuf, obu, obv, f_ref, t_ref, isem, osem
):
    nt, order, w = u_ref.shape
    done = preu_ref.shape[0]
    rest = nt - done

    def copies(t):
        if t < done:
            return [
                pltpu.make_async_copy(preu_ref.at[t], obu.at[t], isem.at[0, t]),
                pltpu.make_async_copy(prev_ref.at[t], obv.at[t], isem.at[1, t]),
            ]
        k = t - done
        return [
            pltpu.make_async_copy(u_ref.at[t], ubuf.at[k], isem.at[0, t]),
            pltpu.make_async_copy(left_ref.at[k], lbuf.at[k], isem.at[1, t]),
            pltpu.make_async_copy(v_ref.at[t], vbuf.at[k], isem.at[2, t]),
        ]

    def store(t):
        return [
            pltpu.make_async_copy(obu.at[t], ou_ref.at[t], osem.at[0, t]),
            pltpu.make_async_copy(obv.at[t], ov_ref.at[t], osem.at[1, t]),
        ]

    loads = [copies(t) for t in range(nt)]
    outs = [store(t) for t in range(nt)]
    for t in range(nt):
        for copy in loads[t]:
            copy.start()

    def cmat(t):
        return jnp.concatenate([a_ref[t], px_ref[...]], axis=0)

    for k in range(rest):
        t_ref[k], f_ref[k] = prepare(cmat(done + k), m_ref[k])
    for t in range(done):
        for copy in loads[t]:
            copy.wait()
        for copy in outs[t]:
            copy.start()
    eliminate(f_ref, 0, rest, w)
    for t in range(done, nt):
        for copy in loads[t]:
            copy.wait()
    for k in range(rest):
        t = done + k
        z, rv = finish(order, trank[t], crank[0], listed[t] == 1, cmat(t), f_ref[k], t_ref[k])
        both = ndot(jnp.concatenate([ubuf[k], lbuf[k]], axis=1), z)
        obu[t] = (both[:, :w] + both[:, w:]).astype(bf16)
        obv[t] = ndot(jnp.concatenate([vbuf[k], x_ref[0]], axis=1), rv).astype(bf16)
        for copy in outs[t]:
            copy.start()
    for tile in outs:
        for copy in tile:
            copy.wait()


def front(mesh_sizes, done, u, v, trank, listed, row_u, row_v, rrank, col_u, col_v, crank, sketch):
    nt, order, w = u.shape
    nz, nc, ny, nx = mesh_sizes
    g = 2
    ng = nt // g
    row_u, row_v = (a.reshape(ng, g, *a.shape[1:]) for a in (row_u, row_v))
    smem = pl.BlockSpec(memory_space=pltpu.SMEM)
    vmem = pl.BlockSpec(memory_space=pltpu.VMEM)
    hbm = pl.BlockSpec(memory_space=pl.ANY)
    dma = pltpu.SemaphoreType.DMA
    return pl.pallas_call(
        functools.partial(gather_kernel, mesh_sizes),
        out_shape=(
            jax.ShapeDtypeStruct((nt - done, 2 * w, 2 * w), f32),
            jax.ShapeDtypeStruct((nt, w, w), bf16),
            jax.ShapeDtypeStruct((w, w), bf16),
            jax.ShapeDtypeStruct((nt - done, order, w), bf16),
            jax.ShapeDtypeStruct((nz, nc, order // (nz * nc), w), bf16),
            jax.ShapeDtypeStruct((done, order, w), bf16),
            jax.ShapeDtypeStruct((done, order, w), bf16),
        ),
        in_specs=[smem, smem, smem, smem, hbm, hbm, hbm, hbm, hbm, hbm, vmem],
        out_specs=(hbm, vmem, vmem, hbm, hbm, hbm, hbm),
        scratch_shapes=[
            pltpu.VMEM((ng, ny, nx, g, w, w), bf16),
            pltpu.VMEM((ng, ny, nx, g, w, w), bf16),
            pltpu.VMEM((2, nz, nc, order // (nz * nc), w), bf16),
            pltpu.VMEM((nt, order, w), bf16),
            pltpu.VMEM((nt, order, w), bf16),
            pltpu.VMEM((nt, order, w), bf16),
            pltpu.VMEM((nt, 2 * w, 2 * w), f32),
            pltpu.VMEM((done, order, w), bf16),
            pltpu.VMEM((done, order, w), bf16),
            pltpu.VMEM((done, 2 * w, 2 * w), bf16),
            pltpu.VMEM((done, 2 * w, w), bf16),
            pltpu.VMEM((done, w, w), f32),
            pltpu.VMEM((done, 2 * w, w), f32),
            dma((4,)),
            dma((2, done)),
            dma((nt,)),
            dma((nt,)),
            dma((nt,)),
            dma((nt,)),
            dma((2, 2, 4)),
            dma((2, 2, 4)),
            dma((ng, 2, 4)),
            dma((ng, 2, 4)),
            dma((2, 4)),
            dma((2, 4)),
            dma((2,)),
            dma((2,)),
        ],
        compiler_params=pltpu.CompilerParams(collective_id=0, has_side_effects=True, vmem_limit_bytes=62 * 1024 * 1024),
    )(trank, rrank, crank, listed, row_u, row_v, col_u, col_v, u, v, sketch)


def back(u, v, trank, listed, crank, m, a, px, left, side_u, pre_u, pre_v):
    nt, order, w = u.shape
    rest = nt - pre_u.shape[0]
    smem = pl.BlockSpec(memory_space=pltpu.SMEM)
    vmem = pl.BlockSpec(memory_space=pltpu.VMEM)
    hbm = pl.BlockSpec(memory_space=pl.ANY)
    return pl.pallas_call(
        back_kernel,
        out_shape=(jax.ShapeDtypeStruct(u.shape, bf16), jax.ShapeDtypeStruct(u.shape, bf16)),
        in_specs=[smem, smem, smem, vmem, vmem, vmem, vmem, hbm, hbm, hbm, hbm, hbm],
        out_specs=(hbm, hbm),
        scratch_shapes=[pltpu.VMEM((rest, order, w), bf16)] * 3
        + [pltpu.VMEM((nt, order, w), bf16)] * 2
        + [
            pltpu.VMEM((rest, w, w), f32),
            pltpu.VMEM((rest, 2 * w, w), f32),
            pltpu.SemaphoreType.DMA((3, nt)),
            pltpu.SemaphoreType.DMA((2, nt)),
        ],
        compiler_params=pltpu.CompilerParams(vmem_limit_bytes=62 * 1024 * 1024),
    )(trank, crank, listed, m, a, px, side_u, u, left, v, pre_u, pre_v)


def on_device(
    sizes, tile_u, tile_v, tile_rank, listed, row_u, row_v, row_rank, col_u, col_v, col_rank, sketch
):
    u, v, trank, flags = tile_u[:, 0], tile_v[:, 0], tile_rank[:, 0], listed[:, 0]
    done = u.shape[0] // 2
    m, a, px, left, side_u, pre_u, pre_v = front(
        sizes, done, u, v, trank, flags, row_u, row_v, row_rank, col_u, col_v, col_rank, sketch
    )
    out_u, out_v = back(u, v, trank, flags, col_rank, m, a, px, left, side_u.reshape(1, *u.shape[1:]), pre_u, pre_v)
    return (out_u[:, None], out_v[:, None])


def solution(mesh):
    return jax.shard_map(
        functools.partial(on_device, (mesh.shape["row"] // 2, 2, 4, mesh.shape["col"] // 4)),
        mesh=mesh,
        in_specs=(
            P("row", "col", None, None),
            P("row", "col", None, None),
            P("row", "col"),
            P("row", "col"),
            P("row", "col", None),
            P("row", "col", None),
            P("row"),
            P("col", "row", None),
            P("col", "row", None),
            P("col"),
            P(),
        ),
        out_specs=(P("row", "col", None, None), P("row", "col", None, None)),
        check_vma=False,
    )
```
